32 devices in a mesh: grp: 1, tm: 16 (over z, y, x), panel: 2 (over core).
Axes of the slice: x: 2, y: 2, z: 4, core: 2. Of those that a mesh axis runs over, the one named last changes fastest.
Arguments:
- series: bfloat16 [8192, 64], P(('grp', 'tm')), may hold values from -4 to 4
- test_matrix: bfloat16 [16384, 512], P('tm', 'panel'), may hold values from -0.046875 to 0.046875
Outputs:
- basis: float32 [8192, 512], P(('grp', 'tm'), 'panel')
- triangle: float32 [512, 512], P('grp', 'panel')
The draws below stay inside these ranges and needn't reach their ends.
All inputs are finite; a program needn't handle non-finite values.
Results may differ from the reference program's by a relative error of at most 0.0003.
Values may be sent and summed in bfloat16 or wider, within the bound.
No kernel may reach another device: no remote copies, remote signals or barrier semaphores. Data moves between devices by JAX's collectives and lax.ppermute only.
A program may use at most 128 MiB of HBM per device.

```python
import math
import jax
import jax.numpy as jnp
from jax import lax

VARS = 64
CH = 512
WINDOW_LAGS = 256
LAG_SPACING = 8
RECORD_STEPS = 8192


period_table = (6, 7, 9, 11, 13, 16, 19, 24, 29, 35, 42, 51, 61, 74, 89, 107, 129, 156, 168, 189, 228, 275, 332, 400, 483, 583, 703, 849, 1024, 1236, 1491, 1800, 2172, 2622, 3164, 3819, 4609, 5563, 6714, 8103, 8766, 10500, 12700, 15300, 18500, 22300, 26900, 32500, 39200, 47300)


def draw_series(key, part):
    components = 48
    streams = jax.random.split(jax.random.fold_in(key, 7), 5)
    table = jnp.asarray(period_table, dtype=jnp.int32)
    chosen = jax.random.randint(streams[0], (components,), 0, len(period_table))
    periods = table[chosen]
    moments = jnp.arange(RECORD_STEPS, dtype=jnp.int32)
    within = moments[:, None] % periods[None, :]
    phases = jax.random.uniform(streams[1], (components,), jnp.float32, 0.0, 2.0 * math.pi)
    angles = 2.0 * math.pi * within.astype(jnp.float32) / periods.astype(jnp.float32)[None, :]
    wave_rows = jnp.sin(angles + phases[None, :])
    levels = jax.random.uniform(streams[2], (components,), jnp.float32)
    amplitude = 0.35 * jnp.exp(-math.log(33.0) * levels)
    mixing = 0.55 * jax.random.normal(streams[3], (components, VARS), jnp.float32)
    signal = jnp.dot(wave_rows * amplitude[None, :], mixing, precision=lax.Precision.HIGHEST)
    fraction = moments.astype(jnp.float32) / float(RECORD_STEPS)
    noise = 0.6 * jax.random.normal(streams[4], (RECORD_STEPS, VARS), jnp.float32)
    envelope = 1.6 * jnp.exp(math.log(4.0) * (fraction - 1.0))
    return jnp.clip((signal + noise) * envelope[:, None], -4.0, 4.0).astype(jnp.bfloat16)


def block_scale(own_key, dims, shards, low, largest):
    gain = 1.0
    for axis_at, blocks in shards:
        draws = jax.random.uniform(jax.random.fold_in(jax.random.fold_in(own_key, 6), axis_at), (blocks,), jnp.float32, low / len(shards), largest / len(shards))
        gain = gain * jnp.repeat(jnp.exp(draws), dims[axis_at] // blocks).reshape((-1,) + (1,) * (len(dims) - 1 - axis_at))
    return gain


def centred(rng, shape, width, limit, cuts=(), kind=jnp.bfloat16):
    drawn = jax.random.normal(rng, shape, jnp.float32) * width
    if len(cuts) > 0:
        drawn = block_scale(rng, shape, cuts, -0.22, 0.18) * drawn
    return jnp.clip(drawn, min=-limit, max=limit).astype(kind)


def setup_inputs(seed: int = 0, part: int = 0) -> dict:
    seeds = jax.random.split(jax.random.key(seed), 3)
    part_splits = jax.random.split(jax.random.fold_in(seeds[2], part), 3)
    return {
        "series": draw_series(jax.random.fold_in(jax.random.fold_in(seeds[2], part), 71), part),
        "test_matrix": centred(seeds[1], (WINDOW_LAGS * VARS, CH), (WINDOW_LAGS * VARS) ** -0.5, 0.046875, ((0, 16), (1, 2))),
    }


def reference(series, test_matrix):
    window_span = LAG_SPACING * (WINDOW_LAGS - 1)
    padded_series = jnp.concatenate([series, jnp.zeros((window_span, VARS), series.dtype)], 0)
    weights = test_matrix.reshape(WINDOW_LAGS, VARS, CH)

    def one_lag(total, lag_number):
        embedded_rows = lax.dynamic_slice_in_dim(padded_series, (lag_number * LAG_SPACING).astype(jnp.int32), RECORD_STEPS, 0)
        piece = lax.dynamic_index_in_dim(weights, lag_number, 0, keepdims=False)
        return (total + jnp.dot(embedded_rows.astype(jnp.float32), piece.astype(jnp.float32), preferred_element_type=jnp.float32), None)
    sketch, _ = lax.scan(one_lag, jnp.zeros((RECORD_STEPS, CH), jnp.float32), jnp.arange(WINDOW_LAGS, dtype=jnp.int32))
    qmat, rmat = jnp.linalg.qr(sketch)
    signs = jnp.where(jnp.diagonal(rmat) < 0, -1.0, 1.0).astype(sketch.dtype)
    qmat = qmat * signs[None, :]
    rmat = rmat * signs[:, None]
    factor = jnp.sqrt(jnp.asarray(RECORD_STEPS, sketch.dtype))
    return (qmat * factor, rmat / factor)
```

```python
import functools
import math

import jax
import jax.numpy as jnp
import numpy as np
from jax import lax
from jax.experimental import pallas as pl
from jax.experimental.pallas import tpu as pltpu
from jax.sharding import PartitionSpec as P

WINDOW_LAGS = 256
LAG_SPACING = 8
NB = 128
IB = 16
TILE = 256
HI = lax.Precision.HIGHEST
BOTH = ("tm", "panel")


def dot_nn(a, b):
    return lax.dot_general(a, b, (((1,), (0,)), ((), ())), precision=HI, preferred_element_type=jnp.float32)


def dot_tn(a, b):
    return lax.dot_general(a, b, (((0,), (0,)), ((), ())), precision=HI, preferred_element_type=jnp.float32)


def dot_nt(a, b):
    return lax.dot_general(a, b, (((1,), (1,)), ((), ())), precision=HI, preferred_element_type=jnp.float32)


class Plan:
    def __init__(self, n):
        lo = 1
        while lo * lo < n:
            lo *= 2
        if n % lo or (n // lo) * lo != n:
            lo = n
        if lo * lo > n and n % (lo // 2) == 0:
            lo //= 2
        self.n, self.lo, self.hi = n, lo, n // lo
        self.mixed = self.lo == self.hi
        self.na, self.nb = self.hi, self.lo

    def index(self, a, b, panel):
        straight = a * self.lo + b
        if not self.mixed:
            return straight
        return (1 - panel) * (b * self.lo + a) + panel * straight

    def coords(self, i, panel):
        hi, lo = i // self.lo, i % self.lo
        if not self.mixed:
            return hi, lo
        return (1 - panel) * lo + panel * hi, (1 - panel) * hi + panel * lo

    def pairs(self, da, db):
        out = []
        for i in range(self.n):
            for panel in range(2):
                a, b = self.coords(i, panel)
                j = self.index((a + da) % self.na, (b + db) % self.nb, panel)
                out.append((i * 2 + panel, j * 2 + panel))
        return out

    def plain_pairs(self, dhi, dlo):
        out = []
        for i in range(self.n):
            hi, lo = i // self.lo, i % self.lo
            out.append((i, ((hi + dhi) % self.hi) * self.lo + (lo + dlo) % self.lo))
        return out


def sketch_kernel(plan, rows, depth, *refs):
    na, nb = plan.na, plan.nb
    stacks = refs[: plan.lo]
    omegas = refs[plan.lo : plan.lo + na]
    outs = refs[plan.lo + na : plan.lo + na + nb]
    flat, wide = refs[plan.lo + na + nb :]
    i = lax.axis_index("tm")
    panel = lax.axis_index("panel")
    hi, lo = i // plan.lo, i % plan.lo
    total = plan.n * rows
    variables = stacks[0].shape[1]
    flat[total:, :] = jnp.zeros((flat.shape[0] - total, variables), flat.dtype)
    for slo in range(plan.lo):

        @pl.loop(0, plan.hi)
        def _(shi):
            slab = lax.rem(hi - shi + plan.hi, plan.hi) * plan.lo + lax.rem(lo - slo + plan.lo, plan.lo)
            flat[pl.ds(pl.multiple_of(slab * rows, rows), rows), :] = stacks[slo][
                pl.ds(pl.multiple_of(shi * rows, rows), rows), :
            ]

    step = 256

    @pl.loop(0, wide.shape[0] // step)
    def _(k):
        start = pl.multiple_of(k * step, step)
        now = flat[pl.ds(start, step + 16), :]
        wide[pl.ds(start, step), :] = jnp.concatenate(
            [now[:step], now[LAG_SPACING : LAG_SPACING + step]], 1
        )

    a, b = plan.coords(i, panel)
    shift = depth // variables * LAG_SPACING
    chunk = min(256, depth)
    for sb in range(nb):
        slab = plan.index(a, lax.rem(b + sb, nb), panel)

        @pl.loop(0, rows // TILE)
        def _(k):
            start = pl.multiple_of(k * TILE, TILE)
            acc = jnp.zeros((TILE, outs[0].shape[1]), jnp.float32)
            for sa in range(na):
                block = plan.index(lax.rem(a - sa + na, na), b, panel)
                base = pl.multiple_of(slab * rows + block * shift + start, 16)
                for first in range(0, depth, chunk):
                    pieces = []
                    for col in range(first, first + chunk, 2 * variables):
                        offset = col // variables * LAG_SPACING
                        pieces.append(wide[pl.ds(base + offset, TILE), :])
                    left = jnp.concatenate(pieces, 1) if len(pieces) > 1 else pieces[0]
                    acc = acc + jnp.dot(
                        left, omegas[sa][first : first + chunk, :], preferred_element_type=jnp.float32
                    )
            outs[sb][pl.ds(start, TILE), :] = acc


def gram_kernel(own_ref, other_ref, out_ref):
    own = own_ref[...]
    half = own.shape[1]
    out_ref[:, :half] = dot_tn(own, own)
    panel = lax.axis_index("panel")

    @pl.when(panel == 0)
    def _():
        out_ref[:, half:] = dot_tn(own_ref[...], other_ref[:, : half // 2])

    @pl.when(panel == 1)
    def _():
        out_ref[:, half:] = dot_tn(other_ref[...], own_ref[:, half // 2 :])


def small_factor(block, base, size):
    cols = [jnp.broadcast_to(block[:, base + j : base + j + 1], (size, NB)) for j in range(size)]
    sub = lax.broadcasted_iota(jnp.int32, (size, NB), 0)
    scale = jnp.zeros((size, NB), jnp.float32)
    left, right = block[:, :NB], block[:, NB:]
    for j in range(size):
        pivot = jnp.broadcast_to(cols[j][j : j + 1, :], (size, NB))
        mult = jnp.where(sub > j, cols[j] * (1.0 / pivot), 0.0)
        for k in range(j + 1, size):
            cols[k] = cols[k] - mult * jnp.broadcast_to(cols[j][k : k + 1, :], (size, NB))
        scale = jnp.where(sub == j, pivot, scale)
        if j < size - 1:
            left = left - mult * jnp.broadcast_to(left[j : j + 1, :], (size, NB))
            right = right - mult * jnp.broadcast_to(right[j : j + 1, :], (size, NB))
    inv = lax.rsqrt(scale)
    return jnp.concatenate([left * inv, right * inv], 1)


def diag_factor(w):
    for kb in range(NB // IB):
        end = (kb + 1) * IB
        rows = small_factor(w[kb * IB : end, :], kb * IB, IB)
        w[kb * IB : end, :] = rows
        if end < NB:
            w[end:, :] = w[end:, :] - dot_tn(rows[:, end:NB], rows)


def factor_kernel(factor, gown, gother, sown, sother, basis_ref, tri_ref, a, w, r, v):
    half = gown.shape[0]
    n = 2 * half
    panel = lax.axis_index("panel")

    def place(first, second):
        a[:half, :half] = first[:, :half]
        a[:half, half : half + half // 2] = first[:, half:]
        a[half:, half:] = second[:, :half]
        a[:half, half + half // 2 :] = second[:, half:]

    @pl.when(panel == 0)
    def _():
        place(gown, gother)

    @pl.when(panel == 1)
    def _():
        place(gother, gown)

    r[...] = jnp.zeros_like(r)
    v[...] = jnp.zeros_like(v)
    ri = lax.broadcasted_iota(jnp.int32, (NB, NB), 0)
    ci = lax.broadcasted_iota(jnp.int32, (NB, NB), 1)
    eye = (ri == ci).astype(jnp.float32)
    for j in range(n // NB):
        js = slice(j * NB, (j + 1) * NB)
        w[:, :NB] = a[js, js]
        w[:, NB:] = eye
        diag_factor(w)
        wj = w[:, NB:]
        r[js, js] = jnp.where(ci >= ri, w[:, :NB], 0.0)
        v[js, js] = wj.T
        if (j + 1) * NB < n:
            rest = slice((j + 1) * NB, n)
            row = dot_nn(wj, a[js, rest])
            r[js, rest] = row
            for i in range(j + 1, n // NB):
                at = (i - j - 1) * NB
                a[i * NB : (i + 1) * NB, i * NB :] = a[i * NB : (i + 1) * NB, i * NB :] - dot_tn(
                    row[:, at : at + NB], row[:, at:]
                )
        if j > 0:
            top = slice(0, j * NB)
            v[top, js] = -dot_nt(dot_nn(v[top, top], r[top, js]), wj)

    @pl.when(panel == 0)
    def _():
        tri_ref[...] = r[:, :half] * (1.0 / factor)
        basis_ref[...] = dot_nn(sown[...], v[:half, :half]) * factor

    @pl.when(panel == 1)
    def _():
        tri_ref[...] = r[:, half:] * (1.0 / factor)
        basis_ref[...] = (dot_nn(sother[...], v[:half, half:]) + dot_nn(sown[...], v[half:, half:])) * factor


def vmem(count):
    return [pl.BlockSpec(memory_space=pltpu.VMEM)] * count


def per_device(series, test_matrix):
    n = lax.axis_size("tm")
    plan = Plan(n)
    rows, variables = series.shape
    depth, half = test_matrix.shape
    gathered = [test_matrix]
    for s in range(1, plan.na):
        gathered.append(lax.ppermute(test_matrix, BOTH, plan.pairs(s, 0)))
    pieces = [series]
    for s in range(1, plan.hi):
        pieces.append(lax.ppermute(series, "tm", plan.plain_pairs(s, 0)))
    stack = jnp.concatenate(pieces, 0)
    stacks = [stack]
    for s in range(1, plan.lo):
        stacks.append(lax.ppermute(stack, "tm", plan.plain_pairs(0, s)))
    span = WINDOW_LAGS * LAG_SPACING
    parts = pl.pallas_call(
        functools.partial(sketch_kernel, plan, rows, depth),
        out_shape=[jax.ShapeDtypeStruct((rows, half), jnp.float32)] * plan.nb,
        in_specs=vmem(plan.lo + plan.na),
        out_specs=vmem(plan.nb),
        scratch_shapes=[
            pltpu.VMEM((n * rows + span + 16, variables), jnp.bfloat16),
            pltpu.VMEM((n * rows + span, 2 * variables), jnp.bfloat16),
        ],
        name="sketch",
    )(*stacks, *gathered)
    own = parts[0]
    arrived = [lax.ppermute(parts[s], BOTH, plan.pairs(0, s)) for s in range(1, plan.nb)]
    for piece in arrived:
        own = own + piece
    other = lax.ppermute(own, "panel", [(0, 1), (1, 0)])
    gram = pl.pallas_call(
        gram_kernel,
        out_shape=jax.ShapeDtypeStruct((half, half + half // 2), jnp.float32),
        in_specs=vmem(2),
        out_specs=vmem(1)[0],
        name="gram",
    )(own, other)
    width = half + half // 2
    spread = lax.all_to_all(gram.reshape(n, half // n, width), "tm", 0, 0, tiled=True)
    summed = jnp.sum(spread, 0)
    wide = jnp.broadcast_to(summed[None], (n, half // n, width))
    gram = lax.all_to_all(wide, "tm", 0, 0, tiled=True).reshape(half, width)
    gram_other = lax.ppermute(gram, "panel", [(0, 1), (1, 0)])
    full = 2 * half
    return tuple(
        pl.pallas_call(
            functools.partial(factor_kernel, math.sqrt(n * rows)),
            out_shape=[
                jax.ShapeDtypeStruct((rows, half), jnp.float32),
                jax.ShapeDtypeStruct((full, half), jnp.float32),
            ],
            in_specs=vmem(4),
            out_specs=vmem(2),
            scratch_shapes=[
                pltpu.VMEM((full, full), jnp.float32),
                pltpu.VMEM((NB, 2 * NB), jnp.float32),
                pltpu.VMEM((full, full), jnp.float32),
                pltpu.VMEM((full, full), jnp.float32),
            ],
            name="factor",
        )(gram, gram_other, own, other)
    )


def solution(mesh):
    placed = (P(("grp", "tm"), None), P("tm", "panel"))
    return jax.shard_map(
        per_device,
        mesh=mesh,
        in_specs=placed,
        out_specs=(P(("grp", "tm"), "panel"), P("grp", "panel")),
        check_vma=False,
    )
```

```python
import functools
import math

import jax
import jax.numpy as jnp
import numpy as np
from jax import lax
from jax.experimental import pallas as pl
from jax.experimental.pallas import tpu as pltpu
from jax.sharding import PartitionSpec as P

WINDOW_LAGS = 256
LAG_SPACING = 8
NB = 128
IB = 16
TILE = 256
HI = lax.Precision.HIGHEST
BOTH = ("tm", "panel")


def dot_nn(a, b):
    return lax.dot_general(a, b, (((1,), (0,)), ((), ())), precision=HI, preferred_element_type=jnp.float32)


def dot_tn(a, b):
    return lax.dot_general(a, b, (((0,), (0,)), ((), ())), precision=HI, preferred_element_type=jnp.float32)


def dot_nt(a, b):
    return lax.dot_general(a, b, (((1,), (1,)), ((), ())), precision=HI, preferred_element_type=jnp.float32)


class Plan:
    def __init__(self, n):
        assert n & (n - 1) == 0
        lo = 1
        while lo * lo * 4 <= n:
            lo *= 2
        self.n, self.lo, self.hi = n, lo, n // lo
        self.mixed = self.lo == self.hi
        self.na, self.nb = self.hi, self.lo

    def index(self, a, b, panel):
        straight = a * self.lo + b
        if not self.mixed:
            return straight
        return (1 - panel) * (b * self.lo + a) + panel * straight

    def coords(self, i, panel):
        hi, lo = i // self.lo, i % self.lo
        if not self.mixed:
            return hi, lo
        return (1 - panel) * lo + panel * hi, (1 - panel) * hi + panel * lo

    def pairs(self, da, db):
        out = []
        for i in range(self.n):
            for panel in range(2):
                a, b = self.coords(i, panel)
                out.append((i * 2 + panel, self.index(a ^ da, b ^ db, panel) * 2 + panel))
        return out

    def plain_pairs(self, dhi, dlo):
        return [(i, (i // self.lo ^ dhi) * self.lo + (i % self.lo ^ dlo)) for i in range(self.n)]


def gather_blocks(plan, block):
    depth = block.shape[0]

    def sent(value, da):
        return lax.ppermute(value, BOTH, plan.pairs(da, 0))

    if plan.na != 4:
        arrays = [block] + [sent(block, s) for s in range(1, plan.na)]
        return arrays, [[(s, 0, depth)] for s in range(plan.na)]
    cut = depth // 2
    top, bottom = block[:cut], block[cut:]
    top_one, bottom_two = sent(top, 1), sent(bottom, 2)
    top_pair = sent(jnp.concatenate([top, top_one], 0), 2)
    bottom_pair = sent(jnp.concatenate([bottom, bottom_two], 0), 1)
    arrays = [block, top_one, bottom_two, top_pair, bottom_pair]
    where = [
        [(0, 0, depth)],
        [(1, 0, cut), (4, 0, cut)],
        [(3, 0, cut), (2, 0, cut)],
        [(3, cut, cut), (4, cut, cut)],
    ]
    return arrays, where


def widen_kernel(plan, rows, *refs):
    stacks = refs[: plan.lo]
    wide, flat = refs[plan.lo :]
    i = lax.axis_index("tm")
    hi, lo = i // plan.lo, i % plan.lo
    total = plan.n * rows
    variables = stacks[0].shape[1]
    flat[total:, :] = jnp.zeros((flat.shape[0] - total, variables), flat.dtype)
    for slo in range(plan.lo):

        @pl.loop(0, plan.hi)
        def _(shi):
            slab = (hi ^ shi) * plan.lo + (lo ^ slo)
            flat[pl.ds(pl.multiple_of(slab * rows, rows), rows), :] = stacks[slo][
                pl.ds(pl.multiple_of(shi * rows, rows), rows), :
            ]

    step = 256

    @pl.loop(0, wide.shape[0] // step)
    def _(k):
        start = pl.multiple_of(k * step, step)
        now = flat[pl.ds(start, step + 16), :]
        wide[pl.ds(start, step), :] = jnp.concatenate(
            [now[:step], now[LAG_SPACING : LAG_SPACING + step]], 1
        )


def sketch_kernel(plan, rows, depth, variables, where, sb, wide, *refs):
    blocks, out = refs[:-1], refs[-1]
    i = lax.axis_index("tm")
    panel = lax.axis_index("panel")
    a, b = plan.coords(i, panel)
    shift = depth // variables * LAG_SPACING
    slab = plan.index(a, b ^ sb, panel)

    @pl.loop(0, rows // TILE)
    def _(k):
        start = pl.multiple_of(k * TILE, TILE)
        acc = jnp.zeros((TILE, out.shape[1]), jnp.float32)
        for sa in range(plan.na):
            block = plan.index(a ^ sa, b, panel)
            base = pl.multiple_of(slab * rows + block * shift + start, 16)
            past = 0
            for array, row, count in where[sa]:
                chunk = min(256, count)
                for first in range(0, count, chunk):
                    pieces = []
                    for col in range(past + first, past + first + chunk, 2 * variables):
                        offset = col // variables * LAG_SPACING
                        pieces.append(wide[pl.ds(base + offset, TILE), :])
                    left = jnp.concatenate(pieces, 1) if len(pieces) > 1 else pieces[0]
                    right = blocks[array][row + first : row + first + chunk, :]
                    acc = acc + jnp.dot(left, right, preferred_element_type=jnp.float32)
                past += count
        out[pl.ds(start, TILE), :] = acc


def gram_kernel(own_ref, other_ref, out_ref):
    own = own_ref[...]
    half = own.shape[1]
    out_ref[:, :half] = dot_tn(own, own)
    panel = lax.axis_index("panel")

    @pl.when(panel == 0)
    def _():
        out_ref[:, half:] = dot_tn(own_ref[...], other_ref[:, : half // 2])

    @pl.when(panel == 1)
    def _():
        out_ref[:, half:] = dot_tn(other_ref[...], own_ref[:, half // 2 :])


def small_factor(block, base, size):
    cols = [jnp.broadcast_to(block[:, base + j : base + j + 1], (size, NB)) for j in range(size)]
    sub = lax.broadcasted_iota(jnp.int32, (size, NB), 0)
    scale = jnp.zeros((size, NB), jnp.float32)
    left, right = block[:, :NB], block[:, NB:]
    for j in range(size):
        pivot = jnp.broadcast_to(cols[j][j : j + 1, :], (size, NB))
        mult = jnp.where(sub > j, cols[j] * (1.0 / pivot), 0.0)
        for k in range(j + 1, size):
            cols[k] = cols[k] - mult * jnp.broadcast_to(cols[j][k : k + 1, :], (size, NB))
        scale = jnp.where(sub == j, pivot, scale)
        if j < size - 1:
            left = left - mult * jnp.broadcast_to(left[j : j + 1, :], (size, NB))
            right = right - mult * jnp.broadcast_to(right[j : j + 1, :], (size, NB))
    inv = lax.rsqrt(scale)
    return jnp.concatenate([left * inv, right * inv], 1)


def diag_factor(w):
    for kb in range(NB // IB):
        end = (kb + 1) * IB
        rows = small_factor(w[kb * IB : end, :], kb * IB, IB)
        w[kb * IB : end, :] = rows
        if end < NB:
            w[end:, :] = w[end:, :] - dot_tn(rows[:, end:NB], rows)


def factor_kernel(factor, gown, gother, sown, sother, basis_ref, tri_ref, a, w, r, v):
    half = gown.shape[0]
    n = 2 * half
    panel = lax.axis_index("panel")

    def place(first, second):
        a[:half, :half] = first[:, :half]
        a[:half, half : half + half // 2] = first[:, half:]
        a[half:, half:] = second[:, :half]
        a[:half, half + half // 2 :] = second[:, half:]

    @pl.when(panel == 0)
    def _():
        place(gown, gother)

    @pl.when(panel == 1)
    def _():
        place(gother, gown)

    r[...] = jnp.zeros_like(r)
    v[...] = jnp.zeros_like(v)
    ri = lax.broadcasted_iota(jnp.int32, (NB, NB), 0)
    ci = lax.broadcasted_iota(jnp.int32, (NB, NB), 1)
    eye = (ri == ci).astype(jnp.float32)
    for j in range(n // NB):
        js = slice(j * NB, (j + 1) * NB)
        w[:, :NB] = a[js, js]
        w[:, NB:] = eye
        diag_factor(w)
        wj = w[:, NB:]
        r[js, js] = jnp.where(ci >= ri, w[:, :NB], 0.0)
        v[js, js] = wj.T
        if (j + 1) * NB < n:
            rest = slice((j + 1) * NB, n)
            row = dot_nn(wj, a[js, rest])
            r[js, rest] = row
            for i in range(j + 1, n // NB):
                at = (i - j - 1) * NB
                a[i * NB : (i + 1) * NB, i * NB :] = a[i * NB : (i + 1) * NB, i * NB :] - dot_tn(
                    row[:, at : at + NB], row[:, at:]
                )
        if j > 0:
            top = slice(0, j * NB)
            v[top, js] = -dot_nt(dot_nn(v[top, top], r[top, js]), wj)

    @pl.when(panel == 0)
    def _():
        tri_ref[...] = r[:, :half] * (1.0 / factor)
        basis_ref[...] = dot_nn(sown[...], v[:half, :half]) * factor

    @pl.when(panel == 1)
    def _():
        tri_ref[...] = r[:, half:] * (1.0 / factor)
        basis_ref[...] = (dot_nn(sother[...], v[:half, half:]) + dot_nn(sown[...], v[half:, half:])) * factor


def vmem(count):
    return [pl.BlockSpec(memory_space=pltpu.VMEM)] * count


def per_device(series, test_matrix):
    n = lax.axis_size("tm")
    plan = Plan(n)
    rows, variables = series.shape
    depth, half = test_matrix.shape
    arrays, where = gather_blocks(plan, test_matrix)
    pieces = [series]
    for s in range(1, plan.hi):
        pieces.append(lax.ppermute(series, "tm", plan.plain_pairs(s, 0)))
    stack = jnp.concatenate(pieces, 0)
    stacks = [stack]
    for s in range(1, plan.lo):
        stacks.append(lax.ppermute(stack, "tm", plan.plain_pairs(0, s)))
    length = n * rows + WINDOW_LAGS * LAG_SPACING
    wide = pl.pallas_call(
        functools.partial(widen_kernel, plan, rows),
        out_shape=jax.ShapeDtypeStruct((length, 2 * variables), jnp.bfloat16),
        in_specs=vmem(plan.lo),
        out_specs=vmem(1)[0],
        scratch_shapes=[pltpu.VMEM((length + 16, variables), jnp.bfloat16)],
        name="widen",
    )(*stacks)

    def part(sb):
        return pl.pallas_call(
            functools.partial(sketch_kernel, plan, rows, depth, variables, where, sb),
            out_shape=jax.ShapeDtypeStruct((rows, half), jnp.float32),
            in_specs=vmem(1 + len(arrays)),
            out_specs=vmem(1)[0],
            name="sketch%d" % sb,
        )(wide, *arrays)

    arrived = [lax.ppermute(part(s), BOTH, plan.pairs(0, s)) for s in reversed(range(1, plan.nb))]
    own = part(0)
    for piece in arrived:
        own = own + piece
    other = lax.ppermute(own, "panel", [(0, 1), (1, 0)])
    gram = pl.pallas_call(
        gram_kernel,
        out_shape=jax.ShapeDtypeStruct((half, half + half // 2), jnp.float32),
        in_specs=vmem(2),
        out_specs=vmem(1)[0],
        name="gram",
    )(own, other)
    width = half + half // 2
    spread = lax.all_to_all(gram.reshape(n, half // n, width), "tm", 0, 0, tiled=True)
    summed = jnp.sum(spread, 0)
    wide = jnp.broadcast_to(summed[None], (n, half // n, width))
    gram = lax.all_to_all(wide, "tm", 0, 0, tiled=True).reshape(half, width)
    gram_other = lax.ppermute(gram, "panel", [(0, 1), (1, 0)])
    full = 2 * half
    return tuple(
        pl.pallas_call(
            functools.partial(factor_kernel, math.sqrt(n * rows)),
            out_shape=[
                jax.ShapeDtypeStruct((rows, half), jnp.float32),
                jax.ShapeDtypeStruct((full, half), jnp.float32),
            ],
            in_specs=vmem(4),
            out_specs=vmem(2),
            scratch_shapes=[
                pltpu.VMEM((full, full), jnp.float32),
                pltpu.VMEM((NB, 2 * NB), jnp.float32),
                pltpu.VMEM((full, full), jnp.float32),
                pltpu.VMEM((full, full), jnp.float32),
            ],
            name="factor",
        )(gram, gram_other, own, other)
    )


def solution(mesh):
    placed = (P(("grp", "tm"), None), P("tm", "panel"))
    return jax.shard_map(
        per_device,
        mesh=mesh,
        in_specs=placed,
        out_specs=(P(("grp", "tm"), "panel"), P("grp", "panel")),
        check_vma=False,
    )
```

```python
import functools
import math

import jax
import jax.numpy as jnp
import numpy as np
from jax import lax
from jax.experimental import pallas as pl
from jax.experimental.pallas import tpu as pltpu
from jax.sharding import PartitionSpec as P

WINDOW_LAGS = 256
LAG_SPACING = 8
NB = 128
IB = 16
TILE = 256
HI = lax.Precision.HIGHEST
BOTH = ("tm", "panel")
SWAP = [(0, 1), (1, 0)]


def dot_nn(a, b):
    return lax.dot_general(a, b, (((1,), (0,)), ((), ())), precision=HI, preferred_element_type=jnp.float32)


def dot_tn(a, b):
    return lax.dot_general(a, b, (((0,), (0,)), ((), ())), precision=HI, preferred_element_type=jnp.float32)


def dot_nt(a, b):
    return lax.dot_general(a, b, (((1,), (1,)), ((), ())), precision=HI, preferred_element_type=jnp.float32)


class Plan:
    def __init__(self, n):
        assert n & (n - 1) == 0
        lo = 1
        while lo * lo * 4 <= n:
            lo *= 2
        self.n, self.lo, self.hi = n, lo, n // lo
        self.mixed = self.lo == self.hi
        self.na, self.nb = self.hi, self.lo

    def index(self, a, b, panel):
        straight = a * self.lo + b
        if not self.mixed:
            return straight
        return (1 - panel) * (b * self.lo + a) + panel * straight

    def coords(self, i, panel):
        hi, lo = i // self.lo, i % self.lo
        if not self.mixed:
            return hi, lo
        return (1 - panel) * lo + panel * hi, (1 - panel) * hi + panel * lo

    def pairs(self, da, db):
        out = []
        for i in range(self.n):
            for panel in range(2):
                a, b = self.coords(i, panel)
                out.append((i * 2 + panel, self.index(a ^ da, b ^ db, panel) * 2 + panel))
        return out

    def plain_pairs(self, dhi, dlo):
        return [(i, (i // self.lo ^ dhi) * self.lo + (i % self.lo ^ dlo)) for i in range(self.n)]


def gather_blocks(plan, block):
    depth = block.shape[0]

    def sent(value, da):
        return lax.ppermute(value, BOTH, plan.pairs(da, 0))

    if plan.na != 4:
        arrays = [block] + [sent(block, s) for s in range(1, plan.na)]
        return arrays, [[(s, 0, depth)] for s in range(plan.na)]
    cut = depth // 2
    top, bottom = block[:cut], block[cut:]
    top_one, bottom_two = sent(top, 1), sent(bottom, 2)
    top_pair = sent(jnp.concatenate([top, top_one], 0), 2)
    bottom_pair = sent(jnp.concatenate([bottom, bottom_two], 0), 1)
    arrays = [block, top_one, bottom_two, top_pair, bottom_pair]
    where = [
        [(0, 0, depth)],
        [(1, 0, cut), (4, 0, cut)],
        [(3, 0, cut), (2, 0, cut)],
        [(3, cut, cut), (4, cut, cut)],
    ]
    return arrays, where


def widen_kernel(series, out, flat):
    rows, variables = series.shape
    count = out.shape[0]
    flat[:rows, :] = series[...]
    flat[rows:, :] = jnp.zeros((flat.shape[0] - rows, variables), flat.dtype)
    start = pl.multiple_of(lax.axis_index("panel") * count, count)
    now = flat[pl.ds(start, count + 16), :]
    out[...] = jnp.concatenate([now[:count], now[LAG_SPACING : LAG_SPACING + count]], 1)


def place_kernel(plan, *refs):
    wide = refs[-1]
    i = lax.axis_index("tm")
    panel = lax.axis_index("panel")
    hi, lo = i // plan.lo, i % plan.lo
    count = refs[0].shape[0] // plan.hi
    rows = 2 * count
    total = plan.n * rows
    variables = wide.shape[1] // 2
    wide[total:, :] = jnp.zeros((wide.shape[0] - total, wide.shape[1]), wide.dtype)
    for side in range(2):
        for slo in range(plan.lo):
            ref = refs[side * plan.lo + slo]

            @pl.loop(0, plan.hi)
            def _(shi):
                slab = (hi ^ shi) * plan.lo + (lo ^ slo)
                first = slab * rows + lax.rem(panel + side, 2) * count
                wide[pl.ds(pl.multiple_of(first, count), count), :] = ref[
                    pl.ds(pl.multiple_of(shi * count, count), count), :
                ]

    @pl.loop(1, plan.n + 1)
    def _(k):
        edge = pl.multiple_of(k * rows, rows)
        after = wide[pl.ds(edge, 16), :]
        before = wide[pl.ds(edge - 16, 16), :]
        right = jnp.concatenate([before[:LAG_SPACING, variables:], after[:LAG_SPACING, :variables]], 0)
        wide[pl.ds(edge - 16, 16), :] = jnp.concatenate([before[:, :variables], right], 1)


def sketch_kernel(plan, rows, depth, variables, where, sb, wide, *refs):
    blocks, out = refs[:-1], refs[-1]
    i = lax.axis_index("tm")
    panel = lax.axis_index("panel")
    a, b = plan.coords(i, panel)
    shift = depth // variables * LAG_SPACING
    slab = plan.index(a, b ^ sb, panel)

    @pl.loop(0, rows // TILE)
    def _(k):
        start = pl.multiple_of(k * TILE, TILE)
        acc = jnp.zeros((TILE, out.shape[1]), jnp.float32)
        for sa in range(plan.na):
            block = plan.index(a ^ sa, b, panel)
            base = pl.multiple_of(slab * rows + block * shift + start, 16)
            past = 0
            for array, row, count in where[sa]:
                chunk = min(256, count)
                for first in range(0, count, chunk):
                    pieces = []
                    for col in range(past + first, past + first + chunk, 2 * variables):
                        offset = col // variables * LAG_SPACING
                        pieces.append(wide[pl.ds(base + offset, TILE), :])
                    left = jnp.concatenate(pieces, 1) if len(pieces) > 1 else pieces[0]
                    right = blocks[array][row + first : row + first + chunk, :]
                    acc = acc + jnp.dot(left, right, preferred_element_type=jnp.float32)
                past += count
        out[pl.ds(start, TILE), :] = acc


def gram_kernel(own_ref, other_ref, out_ref):
    half = own_ref.shape[1]
    first, last = own_ref[:, :NB], own_ref[:, NB:]
    out_ref[:, :half] = dot_tn(first, own_ref[...])
    out_ref[:, half : half + NB] = dot_tn(last, last)
    panel = lax.axis_index("panel")

    def cross(left, right):
        both = dot_tn(left, right)
        out_ref[:, half + NB : half + 2 * NB] = both[:NB]
        out_ref[:, half + 2 * NB :] = both[NB:]

    @pl.when(panel == 0)
    def _():
        cross(own_ref[...], other_ref[:, :NB])

    @pl.when(panel == 1)
    def _():
        cross(other_ref[...], own_ref[:, NB:])


def small_factor(block, base, size):
    cols = [jnp.broadcast_to(block[:, base + j : base + j + 1], (size, NB)) for j in range(size)]
    sub = lax.broadcasted_iota(jnp.int32, (size, NB), 0)
    scale = jnp.zeros((size, NB), jnp.float32)
    left, right = block[:, :NB], block[:, NB:]
    for j in range(size):
        pivot = jnp.broadcast_to(cols[j][j : j + 1, :], (size, NB))
        mult = jnp.where(sub > j, cols[j] * (1.0 / pivot), 0.0)
        for k in range(j + 1, size):
            cols[k] = cols[k] - mult * jnp.broadcast_to(cols[j][k : k + 1, :], (size, NB))
        scale = jnp.where(sub == j, pivot, scale)
        if j < size - 1:
            left = left - mult * jnp.broadcast_to(left[j : j + 1, :], (size, NB))
            right = right - mult * jnp.broadcast_to(right[j : j + 1, :], (size, NB))
    inv = lax.rsqrt(scale)
    return jnp.concatenate([left * inv, right * inv], 1)


def diag_factor(w):
    for kb in range(NB // IB):
        end = (kb + 1) * IB
        rows = small_factor(w[kb * IB : end, :], kb * IB, IB)
        w[kb * IB : end, :] = rows
        if end < NB:
            w[end:, :] = w[end:, :] - dot_tn(rows[:, end:NB], rows)


def factor_kernel(factor, gown, gother, sown, sother, basis_ref, tri_ref, a, w, r, v):
    half = sown.shape[1]
    n = 2 * half
    panel = lax.axis_index("panel")

    def place(first, second):
        for at, piece in ((0, first), (half, second)):
            a[at : at + NB, at : at + half] = piece[:, :half]
            a[at + NB : at + half, at + NB : at + half] = piece[:, half : half + NB]
        for at, piece in ((half, first), (half + NB, second)):
            a[:NB, at : at + NB] = piece[:, half + NB : half + 2 * NB]
            a[NB:half, at : at + NB] = piece[:, half + 2 * NB :]

    @pl.when(panel == 0)
    def _():
        place(gown, gother)

    @pl.when(panel == 1)
    def _():
        place(gother, gown)

    r[...] = jnp.zeros_like(r)
    v[...] = jnp.zeros_like(v)
    ri = lax.broadcasted_iota(jnp.int32, (NB, NB), 0)
    ci = lax.broadcasted_iota(jnp.int32, (NB, NB), 1)
    eye = (ri == ci).astype(jnp.float32)
    for j in range(n // NB):
        js = slice(j * NB, (j + 1) * NB)
        w[:, :NB] = a[js, js]
        w[:, NB:] = eye
        diag_factor(w)
        wj = w[:, NB:]
        r[js, js] = jnp.where(ci >= ri, w[:, :NB], 0.0)
        v[js, js] = wj.T
        if (j + 1) * NB < n:
            rest = slice((j + 1) * NB, n)
            row = dot_nn(wj, a[js, rest])
            r[js, rest] = row
            for i in range(j + 1, n // NB):
                at = (i - j - 1) * NB
                a[i * NB : (i + 1) * NB, i * NB :] = a[i * NB : (i + 1) * NB, i * NB :] - dot_tn(
                    row[:, at : at + NB], row[:, at:]
                )
        if j > 0:
            top = slice(0, j * NB)
            v[top, js] = -dot_nt(dot_nn(v[top, top], r[top, js]), wj)

    @pl.when(panel == 0)
    def _():
        tri_ref[...] = r[:, :half] * (1.0 / factor)
        basis_ref[...] = dot_nn(sown[...], v[:half, :half]) * factor

    @pl.when(panel == 1)
    def _():
        tri_ref[...] = r[:, half:] * (1.0 / factor)
        basis_ref[...] = (dot_nn(sother[...], v[:half, half:]) + dot_nn(sown[...], v[half:, half:])) * factor


def vmem(count):
    return [pl.BlockSpec(memory_space=pltpu.VMEM)] * count


def per_device(series, test_matrix):
    n = lax.axis_size("tm")
    plan = Plan(n)
    rows, variables = series.shape
    depth, half = test_matrix.shape
    arrays, where = gather_blocks(plan, test_matrix)
    own_rows = pl.pallas_call(
        widen_kernel,
        out_shape=jax.ShapeDtypeStruct((rows // 2, 2 * variables), jnp.bfloat16),
        in_specs=vmem(1),
        out_specs=vmem(1)[0],
        scratch_shapes=[pltpu.VMEM((rows + 16, variables), jnp.bfloat16)],
        name="widen",
    )(series)
    pieces = [own_rows]
    for s in range(1, plan.hi):
        pieces.append(lax.ppermute(own_rows, "tm", plan.plain_pairs(s, 0)))
    stack = jnp.concatenate(pieces, 0)
    stacks = [stack]
    for s in range(1, plan.lo):
        stacks.append(lax.ppermute(stack, "tm", plan.plain_pairs(0, s)))
    stacks = stacks + [lax.ppermute(value, "panel", SWAP) for value in stacks]
    length = n * rows + WINDOW_LAGS * LAG_SPACING
    wide = pl.pallas_call(
        functools.partial(place_kernel, plan),
        out_shape=jax.ShapeDtypeStruct((length, 2 * variables), jnp.bfloat16),
        in_specs=vmem(2 * plan.lo),
        out_specs=vmem(1)[0],
        name="place",
    )(*stacks)

    def part(sb):
        return pl.pallas_call(
            functools.partial(sketch_kernel, plan, rows, depth, variables, where, sb),
            out_shape=jax.ShapeDtypeStruct((rows, half), jnp.float32),
            in_specs=vmem(1 + len(arrays)),
            out_specs=vmem(1)[0],
            name="sketch%d" % sb,
        )(wide, *arrays)

    arrived = [lax.ppermute(part(s), BOTH, plan.pairs(0, s)) for s in reversed(range(1, plan.nb))]
    own = part(0)
    for piece in arrived:
        own = own + piece
    other = lax.ppermute(own, "panel", SWAP)
    assert half == 2 * NB
    width = 5 * NB
    gram = pl.pallas_call(
        gram_kernel,
        out_shape=jax.ShapeDtypeStruct((NB, width), jnp.float32),
        in_specs=vmem(2),
        out_specs=vmem(1)[0],
        name="gram",
    )(own, other)
    spread = lax.all_to_all(gram.reshape(n, NB // n, width), "tm", 0, 0, tiled=True)
    summed = jnp.sum(spread, 0)
    alike = jnp.broadcast_to(summed[None], (n, NB // n, width))
    gram = lax.all_to_all(alike, "tm", 0, 0, tiled=True).reshape(NB, width)
    gram_other = lax.ppermute(gram, "panel", SWAP)
    full = 2 * half
    return tuple(
        pl.pallas_call(
            functools.partial(factor_kernel, math.sqrt(n * rows)),
            out_shape=[
                jax.ShapeDtypeStruct((rows, half), jnp.float32),
                jax.ShapeDtypeStruct((full, half), jnp.float32),
            ],
            in_specs=vmem(4),
            out_specs=vmem(2),
            scratch_shapes=[
                pltpu.VMEM((full, full), jnp.float32),
                pltpu.VMEM((NB, 2 * NB), jnp.float32),
                pltpu.VMEM((full, full), jnp.float32),
                pltpu.VMEM((full, full), jnp.float32),
            ],
            name="factor",
        )(gram, gram_other, own, other)
    )


def solution(mesh):
    placed = (P(("grp", "tm"), None), P("tm", "panel"))
    return jax.shard_map(
        per_device,
        mesh=mesh,
        in_specs=placed,
        out_specs=(P(("grp", "tm"), "panel"), P("grp", "panel")),
        check_vma=False,
    )
```

```python
import functools
import math

import jax
import jax.numpy as jnp
import numpy as np
from jax import lax
from jax.experimental import pallas as pl
from jax.experimental.pallas import tpu as pltpu
from jax.sharding import PartitionSpec as P

WINDOW_LAGS = 256
LAG_SPACING = 8
NB = 128
IB = 16
TILE = 256
HI = lax.Precision.HIGHEST
BOTH = ("tm", "panel")
SWAP = [(0, 1), (1, 0)]


def dot_nn(a, b):
    return lax.dot_general(a, b, (((1,), (0,)), ((), ())), precision=HI, preferred_element_type=jnp.float32)


def dot_tn(a, b):
    return lax.dot_general(a, b, (((0,), (0,)), ((), ())), precision=HI, preferred_element_type=jnp.float32)


def dot_nt(a, b):
    return lax.dot_general(a, b, (((1,), (1,)), ((), ())), precision=HI, preferred_element_type=jnp.float32)


class Plan:
    def __init__(self, n):
        assert n & (n - 1) == 0
        lo = 1
        while lo * lo * 4 <= n:
            lo *= 2
        self.n, self.lo, self.hi = n, lo, n // lo
        self.mixed = self.lo == self.hi
        self.na, self.nb = self.hi, self.lo

    def index(self, a, b, panel):
        straight = a * self.lo + b
        if not self.mixed:
            return straight
        return (1 - panel) * (b * self.lo + a) + panel * straight

    def coords(self, i, panel):
        hi, lo = i // self.lo, i % self.lo
        if not self.mixed:
            return hi, lo
        return (1 - panel) * lo + panel * hi, (1 - panel) * hi + panel * lo

    def pairs(self, da, db):
        out = []
        for i in range(self.n):
            for panel in range(2):
                a, b = self.coords(i, panel)
                out.append((i * 2 + panel, self.index(a ^ da, b ^ db, panel) * 2 + panel))
        return out

    def plain_pairs(self, dhi, dlo):
        return [(i, (i // self.lo ^ dhi) * self.lo + (i % self.lo ^ dlo)) for i in range(self.n)]


def gather_blocks(plan, block):
    depth = block.shape[0]

    def sent(value, da):
        return lax.ppermute(value, BOTH, plan.pairs(da, 0))

    if plan.na != 4:
        arrays = [block] + [sent(block, s) for s in range(1, plan.na)]
        return arrays, [[(s, 0, depth)] for s in range(plan.na)]
    cut = depth // 2
    top, bottom = block[:cut], block[cut:]
    top_one, bottom_two = sent(top, 1), sent(bottom, 2)
    top_pair = sent(jnp.concatenate([top, top_one], 0), 2)
    bottom_pair = sent(jnp.concatenate([bottom, bottom_two], 0), 1)
    arrays = [block, top_one, bottom_two, top_pair, bottom_pair]
    where = [
        [(0, 0, depth)],
        [(1, 0, cut), (4, 0, cut)],
        [(3, 0, cut), (2, 0, cut)],
        [(3, cut, cut), (4, cut, cut)],
    ]
    return arrays, where


def widen_kernel(series, out, flat):
    rows, variables = series.shape
    count = out.shape[0]
    flat[:rows, :] = series[...]
    flat[rows:, :] = jnp.zeros((flat.shape[0] - rows, variables), flat.dtype)
    start = pl.multiple_of(lax.axis_index("panel") * count, count)
    now = flat[pl.ds(start, count + 16), :]
    out[...] = jnp.concatenate([now[:count], now[LAG_SPACING : LAG_SPACING + count]], 1)


def place_kernel(plan, moves, *refs):
    stacks = refs[: 2 * plan.lo]
    blocks = refs[2 * plan.lo : -4]
    wide, matrix, record_sem, block_sem = refs[-4:]
    i = lax.axis_index("tm")
    panel = lax.axis_index("panel")
    hi, lo = i // plan.lo, i % plan.lo
    count = stacks[0].shape[0] // plan.hi
    rows = 2 * count
    total = plan.n * rows
    variables = wide.shape[1] // 2

    def record_copy(side, slo, shi):
        slab = (hi ^ shi) * plan.lo + (lo ^ slo)
        first = slab * rows + lax.rem(panel + side, 2) * count
        return pltpu.make_async_copy(
            stacks[side * plan.lo + slo].at[pl.ds(pl.multiple_of(shi * count, count), count), :],
            wide.at[pl.ds(pl.multiple_of(first, count), count), :],
            record_sem.at[(side * plan.lo + slo) * plan.hi + shi],
        )

    copies = []
    for at, (array, row, size, target) in enumerate(moves):
        copies.append(
            pltpu.make_async_copy(
                blocks[array].at[row : row + size, :], matrix.at[target : target + size, :], block_sem.at[at]
            )
        )
    for side in range(2):
        for slo in range(plan.lo):

            @pl.loop(0, plan.hi)
            def _(shi):
                record_copy(side, slo, shi).start()

    for copy in copies:
        copy.start()
    wide[total:, :] = jnp.zeros((wide.shape[0] - total, wide.shape[1]), wide.dtype)
    for side in range(2):
        for slo in range(plan.lo):

            @pl.loop(0, plan.hi)
            def _(shi):
                record_copy(side, slo, shi).wait()

    @pl.loop(1, plan.n + 1)
    def _(k):
        edge = pl.multiple_of(k * rows, rows)
        after = wide[pl.ds(edge, 16), :]
        before = wide[pl.ds(edge - 16, 16), :]
        right = jnp.concatenate([before[:LAG_SPACING, variables:], after[:LAG_SPACING, :variables]], 0)
        wide[pl.ds(edge - 16, 16), :] = jnp.concatenate([before[:, :variables], right], 1)

    for copy in copies:
        copy.wait()


def sketch_kernel(plan, rows, depth, variables, sb, wide, matrix, out):
    i = lax.axis_index("tm")
    panel = lax.axis_index("panel")
    a, b = plan.coords(i, panel)
    shift = depth // variables * LAG_SPACING
    slab = plan.index(a, b ^ sb, panel)
    chunk = min(256, depth)

    @pl.loop(0, rows // TILE)
    def _(k):
        start = pl.multiple_of(k * TILE, TILE)
        acc = jnp.zeros((TILE, out.shape[1]), jnp.float32)
        for sa in range(plan.na):
            block = plan.index(a ^ sa, b, panel)
            base = pl.multiple_of(slab * rows + block * shift + start, 16)
            for first in range(0, depth, chunk):
                pieces = []
                for col in range(first, first + chunk, 2 * variables):
                    offset = col // variables * LAG_SPACING
                    pieces.append(wide[pl.ds(base + offset, TILE), :])
                left = jnp.concatenate(pieces, 1) if len(pieces) > 1 else pieces[0]
                right = matrix[sa * depth + first : sa * depth + first + chunk, :]
                acc = acc + jnp.dot(left, right, preferred_element_type=jnp.float32)
        out[pl.ds(start, TILE), :] = acc


def gram_kernel(own_ref, other_ref, out_ref):
    half = own_ref.shape[1]
    first, last = own_ref[:, :NB], own_ref[:, NB:]
    out_ref[:, :half] = dot_tn(first, own_ref[...])
    out_ref[:, half : half + NB] = dot_tn(last, last)
    panel = lax.axis_index("panel")

    def cross(left, right):
        both = dot_tn(left, right)
        out_ref[:, half + NB : half + 2 * NB] = both[:NB]
        out_ref[:, half + 2 * NB :] = both[NB:]

    @pl.when(panel == 0)
    def _():
        cross(own_ref[...], other_ref[:, :NB])

    @pl.when(panel == 1)
    def _():
        cross(other_ref[...], own_ref[:, NB:])


def small_factor(block, base, size):
    cols = [jnp.broadcast_to(block[:, base + j : base + j + 1], (size, NB)) for j in range(size)]
    sub = lax.broadcasted_iota(jnp.int32, (size, NB), 0)
    scale = jnp.zeros((size, NB), jnp.float32)
    left, right = block[:, :NB], block[:, NB:]
    for j in range(size):
        pivot = jnp.broadcast_to(cols[j][j : j + 1, :], (size, NB))
        mult = jnp.where(sub > j, cols[j] * (1.0 / pivot), 0.0)
        for k in range(j + 1, size):
            cols[k] = cols[k] - mult * jnp.broadcast_to(cols[j][k : k + 1, :], (size, NB))
        scale = jnp.where(sub == j, pivot, scale)
        if j < size - 1:
            left = left - mult * jnp.broadcast_to(left[j : j + 1, :], (size, NB))
            right = right - mult * jnp.broadcast_to(right[j : j + 1, :], (size, NB))
    inv = lax.rsqrt(scale)
    return jnp.concatenate([left * inv, right * inv], 1)


def diag_factor(w):
    for kb in range(NB // IB):
        end = (kb + 1) * IB
        rows = small_factor(w[kb * IB : end, :], kb * IB, IB)
        w[kb * IB : end, :] = rows
        if end < NB:
            w[end:, :] = w[end:, :] - dot_tn(rows[:, end:NB], rows)


def factor_kernel(factor, gown, gother, sown_hbm, sother_hbm, basis_hbm, tri_hbm, *scratch):
    a, w, r, v, sown, sother, basis_ref, tri_ref, sem = scratch
    own_in = pltpu.make_async_copy(sown_hbm, sown, sem.at[0])
    other_in = pltpu.make_async_copy(sother_hbm, sother, sem.at[1])
    own_in.start()
    other_in.start()
    half = sown.shape[1]
    n = 2 * half
    panel = lax.axis_index("panel")

    def place(first, second):
        for at, piece in ((0, first), (half, second)):
            a[at : at + NB, at : at + half] = piece[:, :half]
            a[at + NB : at + half, at + NB : at + half] = piece[:, half : half + NB]
        for at, piece in ((half, first), (half + NB, second)):
            a[:NB, at : at + NB] = piece[:, half + NB : half + 2 * NB]
            a[NB:half, at : at + NB] = piece[:, half + 2 * NB :]

    @pl.when(panel == 0)
    def _():
        place(gown, gother)

    @pl.when(panel == 1)
    def _():
        place(gother, gown)

    r[...] = jnp.zeros_like(r)
    v[...] = jnp.zeros_like(v)
    ri = lax.broadcasted_iota(jnp.int32, (NB, NB), 0)
    ci = lax.broadcasted_iota(jnp.int32, (NB, NB), 1)
    eye = (ri == ci).astype(jnp.float32)
    for j in range(n // NB):
        js = slice(j * NB, (j + 1) * NB)
        w[:, :NB] = a[js, js]
        w[:, NB:] = eye
        diag_factor(w)
        wj = w[:, NB:]
        r[js, js] = jnp.where(ci >= ri, w[:, :NB], 0.0)
        v[js, js] = wj.T
        if (j + 1) * NB < n:
            rest = slice((j + 1) * NB, n)
            row = dot_nn(wj, a[js, rest])
            r[js, rest] = row
            for i in range(j + 1, n // NB):
                at = (i - j - 1) * NB
                a[i * NB : (i + 1) * NB, i * NB :] = a[i * NB : (i + 1) * NB, i * NB :] - dot_tn(
                    row[:, at : at + NB], row[:, at:]
                )
        if j > 0:
            top = slice(0, j * NB)
            v[top, js] = -dot_nt(dot_nn(v[top, top], r[top, js]), wj)

    @pl.when(panel == 0)
    def _():
        tri_ref[...] = r[:, :half] * (1.0 / factor)

    @pl.when(panel == 1)
    def _():
        tri_ref[...] = r[:, half:] * (1.0 / factor)

    tri_out = pltpu.make_async_copy(tri_ref, tri_hbm, sem.at[2])
    tri_out.start()
    own_in.wait()
    other_in.wait()
    outs = []
    piece = basis_ref.shape[0] // 2
    for part in range(2):
        at = slice(part * piece, (part + 1) * piece)

        @pl.when(panel == 0)
        def _():
            basis_ref[at, :] = dot_nn(sown[at, :], v[:half, :half] * factor)

        @pl.when(panel == 1)
        def _():
            basis_ref[at, :] = dot_nn(sother[at, :], v[:half, half:] * factor) + dot_nn(
                sown[at, :], v[half:, half:] * factor
            )

        outs.append(pltpu.make_async_copy(basis_ref.at[at, :], basis_hbm.at[at, :], sem.at[3 + part]))
        outs[-1].start()
    tri_out.wait()
    for out in outs:
        out.wait()


def vmem(count):
    return [pl.BlockSpec(memory_space=pltpu.VMEM)] * count


def scoped(mebibytes):
    return pltpu.CompilerParams(vmem_limit_bytes=mebibytes << 20)


def anywhere(count):
    return [pl.BlockSpec(memory_space=pl.ANY)] * count


def in_vmem(value):
    return pltpu.with_memory_space_constraint(value, pltpu.VMEM)


def per_device(series, test_matrix):
    n = lax.axis_size("tm")
    plan = Plan(n)
    rows, variables = series.shape
    depth, half = test_matrix.shape
    arrays, where = gather_blocks(plan, test_matrix)
    own_rows = pl.pallas_call(
        widen_kernel,
        out_shape=jax.ShapeDtypeStruct((rows // 2, 2 * variables), jnp.bfloat16),
        in_specs=vmem(1),
        out_specs=vmem(1)[0],
        scratch_shapes=[pltpu.VMEM((rows + 16, variables), jnp.bfloat16)],
        name="widen",
        compiler_params=scoped(8),
    )(series)
    pieces = [own_rows]
    for s in range(1, plan.hi):
        pieces.append(lax.ppermute(own_rows, "tm", plan.plain_pairs(s, 0)))
    stack = jnp.concatenate(pieces, 0)
    stacks = [stack]
    for s in range(1, plan.lo):
        stacks.append(lax.ppermute(stack, "tm", plan.plain_pairs(0, s)))
    stacks = stacks + [lax.ppermute(value, "panel", SWAP) for value in stacks]
    length = n * rows + WINDOW_LAGS * LAG_SPACING
    moves = []
    for s, parts in enumerate(where):
        target = s * depth
        for array, row, size in parts:
            moves.append((array, row, size, target))
            target += size
    wide, matrix = pl.pallas_call(
        functools.partial(place_kernel, plan, moves),
        out_shape=[
            pltpu.VMEM((length, 2 * variables), jnp.bfloat16),
            pltpu.VMEM((plan.na * depth, half), jnp.bfloat16),
        ],
        in_specs=anywhere(len(stacks) + len(arrays)),
        out_specs=vmem(2),
        scratch_shapes=[pltpu.SemaphoreType.DMA((2 * n,)), pltpu.SemaphoreType.DMA((len(moves),))],
        name="place",
        compiler_params=scoped(8),
    )(*stacks, *arrays)
    wide, matrix = in_vmem(wide), in_vmem(matrix)

    def part(sb):
        return pl.pallas_call(
            functools.partial(sketch_kernel, plan, rows, depth, variables, sb),
            out_shape=jax.ShapeDtypeStruct((rows, half), jnp.float32),
            in_specs=vmem(2),
            out_specs=vmem(1)[0],
            name="sketch%d" % sb,
            compiler_params=scoped(8),
            cost_estimate=pl.CostEstimate(
                flops=2 * rows * plan.na * depth * half, bytes_accessed=4 * rows * half, transcendentals=0
            ),
        )(wide, matrix)

    arrived = [lax.ppermute(part(s), BOTH, plan.pairs(0, s)) for s in reversed(range(1, plan.nb))]
    own = part(0)
    for piece in arrived:
        own = own + piece
    other = lax.ppermute(own, "panel", SWAP)
    assert half == 2 * NB
    width = 5 * NB
    gram = pl.pallas_call(
        gram_kernel,
        out_shape=jax.ShapeDtypeStruct((NB, width), jnp.float32),
        in_specs=vmem(2),
        out_specs=vmem(1)[0],
        name="gram",
        compiler_params=scoped(16),
    )(in_vmem(own), in_vmem(other))
    spread = lax.all_to_all(gram.reshape(n, NB // n, width), "tm", 0, 0, tiled=True)
    summed = jnp.sum(spread, 0)
    alike = jnp.broadcast_to(summed[None], (n, NB // n, width))
    gram = lax.all_to_all(alike, "tm", 0, 0, tiled=True).reshape(NB, width)
    gram_other = lax.ppermute(gram, "panel", SWAP)
    full = 2 * half
    return tuple(
        pl.pallas_call(
            functools.partial(factor_kernel, math.sqrt(n * rows)),
            out_shape=[
                jax.ShapeDtypeStruct((rows, half), jnp.float32),
                jax.ShapeDtypeStruct((full, half), jnp.float32),
            ],
            in_specs=vmem(2) + anywhere(2),
            out_specs=anywhere(2),
            scratch_shapes=[
                pltpu.VMEM((full, full), jnp.float32),
                pltpu.VMEM((NB, 2 * NB), jnp.float32),
                pltpu.VMEM((full, full), jnp.float32),
                pltpu.VMEM((full, full), jnp.float32),
                pltpu.VMEM((rows, half), jnp.float32),
                pltpu.VMEM((rows, half), jnp.float32),
                pltpu.VMEM((rows, half), jnp.float32),
                pltpu.VMEM((full, half), jnp.float32),
                pltpu.SemaphoreType.DMA((5,)),
            ],
            name="factor",
            compiler_params=scoped(24),
        )(gram, gram_other, own, other)
    )


def solution(mesh):
    placed = (P(("grp", "tm"), None), P("tm", "panel"))
    return jax.shard_map(
        per_device,
        mesh=mesh,
        in_specs=placed,
        out_specs=(P(("grp", "tm"), "panel"), P("grp", "panel")),
        check_vma=False,
    )
```

```python
import functools
import math

import jax
import jax.numpy as jnp
import numpy as np
from jax import lax
from jax.experimental import pallas as pl
from jax.experimental.pallas import tpu as pltpu
from jax.sharding import PartitionSpec as P

WINDOW_LAGS = 256
LAG_SPACING = 8
NB = 128
IB = 16
TILE = 256
HI = lax.Precision.HIGHEST
BOTH = ("tm", "panel")
SWAP = [(0, 1), (1, 0)]


def dot_nn(a, b):
    return lax.dot_general(a, b, (((1,), (0,)), ((), ())), precision=HI, preferred_element_type=jnp.float32)


def dot_tn(a, b):
    return lax.dot_general(a, b, (((0,), (0,)), ((), ())), precision=HI, preferred_element_type=jnp.float32)


def dot_nt(a, b):
    return lax.dot_general(a, b, (((1,), (1,)), ((), ())), precision=HI, preferred_element_type=jnp.float32)


class Plan:
    def __init__(self, n):
        assert n & (n - 1) == 0
        lo = 1
        while lo * lo * 4 <= n:
            lo *= 2
        self.n, self.lo, self.hi = n, lo, n // lo
        self.mixed = self.lo == self.hi
        self.na, self.nb = self.hi, self.lo

    def index(self, a, b, panel):
        straight = a * self.lo + b
        if not self.mixed:
            return straight
        return (1 - panel) * (b * self.lo + a) + panel * straight

    def coords(self, i, panel):
        hi, lo = i // self.lo, i % self.lo
        if not self.mixed:
            return hi, lo
        return (1 - panel) * lo + panel * hi, (1 - panel) * hi + panel * lo

    def pairs(self, da, db):
        out = []
        for i in range(self.n):
            for panel in range(2):
                a, b = self.coords(i, panel)
                out.append((i * 2 + panel, self.index(a ^ da, b ^ db, panel) * 2 + panel))
        return out

    def plain_pairs(self, dhi, dlo):
        return [(i, (i // self.lo ^ dhi) * self.lo + (i % self.lo ^ dlo)) for i in range(self.n)]


def gather_blocks(plan, block):
    depth = block.shape[0]

    def sent(value, da):
        return lax.ppermute(value, BOTH, plan.pairs(da, 0))

    if plan.na != 4:
        arrays = [block] + [sent(block, s) for s in range(1, plan.na)]
        return arrays, [[(s, 0, depth)] for s in range(plan.na)]
    cut = depth // 2
    one, two = sent(block, 1), sent(block, 2)
    top, bottom = sent(one[:cut], 2), sent(two[cut:], 1)
    return [block, one, two, top, bottom], [
        [(0, 0, depth)],
        [(1, 0, depth)],
        [(2, 0, depth)],
        [(3, 0, cut), (4, 0, cut)],
    ]


def scatter_sums(plan, part):
    def sent(value, db):
        return lax.ppermute(value, BOTH, plan.pairs(0, db))

    if plan.nb != 4:
        arrived = [sent(part(s), s) for s in range(1, plan.nb)]
        own = part(0)
    else:
        third = part(3)
        cut = third.shape[0] // 2
        top, bottom = sent(third[:cut], 1), sent(third[cut:], 2)
        two, one = part(2), part(1)
        two = jnp.concatenate([two[:cut] + top, two[cut:]], 0)
        one = jnp.concatenate([one[:cut], one[cut:] + bottom], 0)
        arrived = [sent(two, 2), sent(one, 1)]
        own = part(0)
    for piece in arrived:
        own = own + piece
    return own


def widen_kernel(series, out, flat):
    rows, variables = series.shape
    count = out.shape[0]
    flat[:rows, :] = series[...]
    flat[rows:, :] = jnp.zeros((flat.shape[0] - rows, variables), flat.dtype)
    start = pl.multiple_of(lax.axis_index("panel") * count, count)
    now = flat[pl.ds(start, count + 16), :]
    out[...] = jnp.concatenate([now[:count], now[LAG_SPACING : LAG_SPACING + count]], 1)


def place_kernel(plan, *refs):
    stacks = refs[:-2]
    wide, record_sem = refs[-2:]
    i = lax.axis_index("tm")
    panel = lax.axis_index("panel")
    hi, lo = i // plan.lo, i % plan.lo
    count = stacks[0].shape[0] // plan.hi
    rows = 2 * count
    total = plan.n * rows
    variables = wide.shape[1] // 2

    def record_copy(side, slo, shi):
        slab = (hi ^ shi) * plan.lo + (lo ^ slo)
        first = slab * rows + lax.rem(panel + side, 2) * count
        return pltpu.make_async_copy(
            stacks[side * plan.lo + slo].at[pl.ds(pl.multiple_of(shi * count, count), count), :],
            wide.at[pl.ds(pl.multiple_of(first, count), count), :],
            record_sem.at[(side * plan.lo + slo) * plan.hi + shi],
        )

    for side in range(2):
        for slo in range(plan.lo):

            @pl.loop(0, plan.hi)
            def _(shi):
                record_copy(side, slo, shi).start()

    wide[total:, :] = jnp.zeros((wide.shape[0] - total, wide.shape[1]), wide.dtype)
    for side in range(2):
        for slo in range(plan.lo):

            @pl.loop(0, plan.hi)
            def _(shi):
                record_copy(side, slo, shi).wait()

    @pl.loop(1, plan.n + 1)
    def _(k):
        edge = pl.multiple_of(k * rows, rows)
        after = wide[pl.ds(edge, 16), :]
        before = wide[pl.ds(edge - 16, 16), :]
        right = jnp.concatenate([before[:LAG_SPACING, variables:], after[:LAG_SPACING, :variables]], 0)
        wide[pl.ds(edge - 16, 16), :] = jnp.concatenate([before[:, :variables], right], 1)


def sketch_kernel(plan, rows, depth, variables, where, sb, wide, *refs):
    blocks, out = refs[:-1], refs[-1]
    i = lax.axis_index("tm")
    panel = lax.axis_index("panel")
    a, b = plan.coords(i, panel)
    shift = depth // variables * LAG_SPACING
    slab = plan.index(a, b ^ sb, panel)

    @pl.loop(0, rows // TILE)
    def _(k):
        start = pl.multiple_of(k * TILE, TILE)
        acc = jnp.zeros((TILE, out.shape[1]), jnp.float32)
        for sa in range(plan.na):
            block = plan.index(a ^ sa, b, panel)
            base = pl.multiple_of(slab * rows + block * shift + start, 16)
            past = 0
            for array, row, count in where[sa]:
                chunk = min(256, count)
                for first in range(0, count, chunk):
                    pieces = []
                    for col in range(past + first, past + first + chunk, 2 * variables):
                        offset = col // variables * LAG_SPACING
                        pieces.append(wide[pl.ds(base + offset, TILE), :])
                    left = jnp.concatenate(pieces, 1) if len(pieces) > 1 else pieces[0]
                    right = blocks[array][row + first : row + first + chunk, :]
                    acc = acc + jnp.dot(left, right, preferred_element_type=jnp.float32)
                past += count
        out[pl.ds(start, TILE), :] = acc


def gram_kernel(own_ref, other_ref, out_ref):
    half = own_ref.shape[1]
    first, last = own_ref[:, :NB], own_ref[:, NB:]
    out_ref[:, :half] = dot_tn(first, own_ref[...])
    out_ref[:, half : half + NB] = dot_tn(last, last)
    panel = lax.axis_index("panel")

    def cross(left, right):
        both = dot_tn(left, right)
        out_ref[:, half + NB : half + 2 * NB] = both[:NB]
        out_ref[:, half + 2 * NB :] = both[NB:]

    @pl.when(panel == 0)
    def _():
        cross(own_ref[...], other_ref[:, :NB])

    @pl.when(panel == 1)
    def _():
        cross(other_ref[...], own_ref[:, NB:])


def small_factor(block, base, size):
    cols = [jnp.broadcast_to(block[:, base + j : base + j + 1], (size, NB)) for j in range(size)]
    sub = lax.broadcasted_iota(jnp.int32, (size, NB), 0)
    scale = jnp.zeros((size, NB), jnp.float32)
    left, right = block[:, :NB], block[:, NB:]
    for j in range(size):
        pivot = jnp.broadcast_to(cols[j][j : j + 1, :], (size, NB))
        mult = jnp.where(sub > j, cols[j] * (1.0 / pivot), 0.0)
        for k in range(j + 1, size):
            cols[k] = cols[k] - mult * jnp.broadcast_to(cols[j][k : k + 1, :], (size, NB))
        scale = jnp.where(sub == j, pivot, scale)
        if j < size - 1:
            left = left - mult * jnp.broadcast_to(left[j : j + 1, :], (size, NB))
            right = right - mult * jnp.broadcast_to(right[j : j + 1, :], (size, NB))
    inv = lax.rsqrt(scale)
    return jnp.concatenate([left * inv, right * inv], 1)


def diag_factor(w):
    for kb in range(NB // IB):
        end = (kb + 1) * IB
        rows = small_factor(w[kb * IB : end, :], kb * IB, IB)
        w[kb * IB : end, :] = rows
        if end < NB:
            w[end:, :] = w[end:, :] - dot_tn(rows[:, end:NB], rows)


def factor_kernel(factor, gown, gother, sown_hbm, sother_hbm, basis_hbm, tri_hbm, *scratch):
    a, w, r, v, sown, sother, basis_ref, tri_ref, sem = scratch
    own_in = pltpu.make_async_copy(sown_hbm, sown, sem.at[0])
    other_in = pltpu.make_async_copy(sother_hbm, sother, sem.at[1])
    own_in.start()
    other_in.start()
    half = sown.shape[1]
    n = 2 * half
    panel = lax.axis_index("panel")

    def place(first, second):
        for at, piece in ((0, first), (half, second)):
            a[at : at + NB, at : at + half] = piece[:, :half]
            a[at + NB : at + half, at + NB : at + half] = piece[:, half : half + NB]
        for at, piece in ((half, first), (half + NB, second)):
            a[:NB, at : at + NB] = piece[:, half + NB : half + 2 * NB]
            a[NB:half, at : at + NB] = piece[:, half + 2 * NB :]

    @pl.when(panel == 0)
    def _():
        place(gown, gother)

    @pl.when(panel == 1)
    def _():
        place(gother, gown)

    r[...] = jnp.zeros_like(r)
    v[...] = jnp.zeros_like(v)
    ri = lax.broadcasted_iota(jnp.int32, (NB, NB), 0)
    ci = lax.broadcasted_iota(jnp.int32, (NB, NB), 1)
    eye = (ri == ci).astype(jnp.float32)
    for j in range(n // NB):
        js = slice(j * NB, (j + 1) * NB)
        w[:, :NB] = a[js, js]
        w[:, NB:] = eye
        diag_factor(w)
        wj = w[:, NB:]
        r[js, js] = jnp.where(ci >= ri, w[:, :NB], 0.0)
        v[js, js] = wj.T
        if (j + 1) * NB < n:
            rest = slice((j + 1) * NB, n)
            row = dot_nn(wj, a[js, rest])
            r[js, rest] = row
            for i in range(j + 1, n // NB):
                at = (i - j - 1) * NB
                a[i * NB : (i + 1) * NB, i * NB :] = a[i * NB : (i + 1) * NB, i * NB :] - dot_tn(
                    row[:, at : at + NB], row[:, at:]
                )
        if j > 0:
            top = slice(0, j * NB)
            v[top, js] = -dot_nt(dot_nn(v[top, top], r[top, js]), wj)

    @pl.when(panel == 0)
    def _():
        tri_ref[...] = r[:, :half] * (1.0 / factor)

    @pl.when(panel == 1)
    def _():
        tri_ref[...] = r[:, half:] * (1.0 / factor)

    tri_out = pltpu.make_async_copy(tri_ref, tri_hbm, sem.at[2])
    tri_out.start()
    own_in.wait()
    other_in.wait()
    outs = []
    piece = basis_ref.shape[0] // 2
    for part in range(2):
        at = slice(part * piece, (part + 1) * piece)

        @pl.when(panel == 0)
        def _():
            basis_ref[at, :] = dot_nn(sown[at, :], v[:half, :half] * factor)

        @pl.when(panel == 1)
        def _():
            basis_ref[at, :] = dot_nn(sother[at, :], v[:half, half:] * factor) + dot_nn(
                sown[at, :], v[half:, half:] * factor
            )

        outs.append(pltpu.make_async_copy(basis_ref.at[at, :], basis_hbm.at[at, :], sem.at[3 + part]))
        outs[-1].start()
    tri_out.wait()
    for out in outs:
        out.wait()


def vmem(count):
    return [pl.BlockSpec(memory_space=pltpu.VMEM)] * count


def scoped(mebibytes):
    return pltpu.CompilerParams(vmem_limit_bytes=mebibytes << 20)


def anywhere(count):
    return [pl.BlockSpec(memory_space=pl.ANY)] * count


def in_vmem(value):
    return pltpu.with_memory_space_constraint(value, pltpu.VMEM)


def per_device(series, test_matrix):
    n = lax.axis_size("tm")
    plan = Plan(n)
    rows, variables = series.shape
    depth, half = test_matrix.shape
    arrays, where = gather_blocks(plan, test_matrix)
    own_rows = pl.pallas_call(
        widen_kernel,
        out_shape=jax.ShapeDtypeStruct((rows // 2, 2 * variables), jnp.bfloat16),
        in_specs=vmem(1),
        out_specs=vmem(1)[0],
        scratch_shapes=[pltpu.VMEM((rows + 16, variables), jnp.bfloat16)],
        name="widen",
        compiler_params=scoped(8),
    )(series)
    pieces = [own_rows]
    for s in range(1, plan.hi):
        pieces.append(lax.ppermute(own_rows, "tm", plan.plain_pairs(s, 0)))
    stack = jnp.concatenate(pieces, 0)
    stacks = [stack]
    for s in range(1, plan.lo):
        stacks.append(lax.ppermute(stack, "tm", plan.plain_pairs(0, s)))
    if plan.na == 4:
        stacks = lax.optimization_barrier((stacks, arrays[1], arrays[2]))[0]
    stacks = stacks + [lax.ppermute(value, "panel", SWAP) for value in stacks]
    length = n * rows + WINDOW_LAGS * LAG_SPACING
    wide = pl.pallas_call(
        functools.partial(place_kernel, plan),
        out_shape=pltpu.VMEM((length, 2 * variables), jnp.bfloat16),
        in_specs=anywhere(len(stacks)),
        out_specs=vmem(1)[0],
        scratch_shapes=[pltpu.SemaphoreType.DMA((2 * n,))],
        name="place",
        compiler_params=scoped(8),
    )(*stacks)
    wide = in_vmem(wide)
    arrays = [in_vmem(value) for value in arrays]

    def part(sb):
        return pl.pallas_call(
            functools.partial(sketch_kernel, plan, rows, depth, variables, where, sb),
            out_shape=jax.ShapeDtypeStruct((rows, half), jnp.float32),
            in_specs=vmem(1 + len(arrays)),
            out_specs=vmem(1)[0],
            name="sketch%d" % sb,
            compiler_params=scoped(8),
            cost_estimate=pl.CostEstimate(
                flops=2 * rows * plan.na * depth * half, bytes_accessed=4 * rows * half, transcendentals=0
            ),
        )(wide, *arrays)

    own = scatter_sums(plan, part)
    other = lax.ppermute(own, "panel", SWAP)
    assert half == 2 * NB
    width = 5 * NB
    gram = pl.pallas_call(
        gram_kernel,
        out_shape=jax.ShapeDtypeStruct((NB, width), jnp.float32),
        in_specs=vmem(2),
        out_specs=vmem(1)[0],
        name="gram",
        compiler_params=scoped(16),
    )(in_vmem(own), in_vmem(other))
    spread = lax.all_to_all(gram.reshape(n, NB // n, width), "tm", 0, 0, tiled=True)
    summed = jnp.sum(spread, 0)
    alike = jnp.broadcast_to(summed[None], (n, NB // n, width))
    gram = lax.all_to_all(alike, "tm", 0, 0, tiled=True).reshape(NB, width)
    gram_other = lax.ppermute(gram, "panel", SWAP)
    full = 2 * half
    return tuple(
        pl.pallas_call(
            functools.partial(factor_kernel, math.sqrt(n * rows)),
            out_shape=[
                jax.ShapeDtypeStruct((rows, half), jnp.float32),
                jax.ShapeDtypeStruct((full, half), jnp.float32),
            ],
            in_specs=vmem(2) + anywhere(2),
            out_specs=anywhere(2),
            scratch_shapes=[
                pltpu.VMEM((full, full), jnp.float32),
                pltpu.VMEM((NB, 2 * NB), jnp.float32),
                pltpu.VMEM((full, full), jnp.float32),
                pltpu.VMEM((full, full), jnp.float32),
                pltpu.VMEM((rows, half), jnp.float32),
                pltpu.VMEM((rows, half), jnp.float32),
                pltpu.VMEM((rows, half), jnp.float32),
                pltpu.VMEM((full, half), jnp.float32),
                pltpu.SemaphoreType.DMA((5,)),
            ],
            name="factor",
            compiler_params=scoped(24),
        )(gram, gram_other, own, other)
    )


def solution(mesh):
    placed = (P(("grp", "tm"), None), P("tm", "panel"))
    return jax.shard_map(
        per_device,
        mesh=mesh,
        in_specs=placed,
        out_specs=(P(("grp", "tm"), "panel"), P("grp", "panel")),
        check_vma=False,
    )
```

```python
import functools
import math

import jax
import jax.numpy as jnp
import numpy as np
from jax import lax
from jax.experimental import pallas as pl
from jax.experimental.pallas import tpu as pltpu
from jax.sharding import PartitionSpec as P

WINDOW_LAGS = 256
LAG_SPACING = 8
NB = 128
IB = 16
TILE = 256
HI = lax.Precision.HIGHEST
BOTH = ("tm", "panel")
SWAP = [(0, 1), (1, 0)]


def dot_nn(a, b):
    return lax.dot_general(a, b, (((1,), (0,)), ((), ())), precision=HI, preferred_element_type=jnp.float32)


def dot_tn(a, b):
    return lax.dot_general(a, b, (((0,), (0,)), ((), ())), precision=HI, preferred_element_type=jnp.float32)


def dot_nt(a, b):
    return lax.dot_general(a, b, (((1,), (1,)), ((), ())), precision=HI, preferred_element_type=jnp.float32)


class Plan:
    def __init__(self, n):
        assert n & (n - 1) == 0
        lo = 1
        while lo * lo * 4 <= n:
            lo *= 2
        self.n, self.lo, self.hi = n, lo, n // lo
        self.mixed = self.lo == self.hi
        self.na, self.nb = self.hi, self.lo

    def index(self, a, b, panel):
        straight = a * self.lo + b
        if not self.mixed:
            return straight
        return (1 - panel) * (b * self.lo + a) + panel * straight

    def coords(self, i, panel):
        hi, lo = i // self.lo, i % self.lo
        if not self.mixed:
            return hi, lo
        return (1 - panel) * lo + panel * hi, (1 - panel) * hi + panel * lo

    def pairs(self, da, db):
        out = []
        for i in range(self.n):
            for panel in range(2):
                a, b = self.coords(i, panel)
                out.append((i * 2 + panel, self.index(a ^ da, b ^ db, panel) * 2 + panel))
        return out

    def plain_pairs(self, dhi, dlo):
        return [(i, (i // self.lo ^ dhi) * self.lo + (i % self.lo ^ dlo)) for i in range(self.n)]


def gather_blocks(plan, block):
    depth = block.shape[0]

    def sent(value, da):
        return lax.ppermute(value, BOTH, plan.pairs(da, 0))

    if plan.na != 4:
        arrays = [block] + [sent(block, s) for s in range(1, plan.na)]
        return arrays, [[(s, 0, depth)] for s in range(plan.na)]
    cut = depth // 2
    one, two = sent(block, 1), sent(block, 2)
    top, bottom = sent(one[:cut], 2), sent(two[cut:], 1)
    return [block, one, two, top, bottom], [
        [(0, 0, depth)],
        [(1, 0, depth)],
        [(2, 0, depth)],
        [(3, 0, cut), (4, 0, cut)],
    ]


def scatter_sums(plan, part):
    def sent(value, db):
        return lax.ppermute(value, BOTH, plan.pairs(0, db))

    if plan.nb != 4:
        arrived = [sent(part(s), s) for s in range(1, plan.nb)]
        own = part(0)
    else:
        third = part(3)
        cut = third.shape[0] // 2
        top, bottom = sent(third[:cut], 1), sent(third[cut:], 2)
        two, one = part(2), part(1)
        two = jnp.concatenate([two[:cut] + top, two[cut:]], 0)
        one = jnp.concatenate([one[:cut], one[cut:] + bottom], 0)
        arrived = [sent(two, 2), sent(one, 1)]
        own = part(0)
    for piece in arrived:
        own = own + piece
    return own


def pack_kernel(series, out):
    count = 2 * out.shape[0]
    variables = series.shape[1]
    start = pl.multiple_of(lax.axis_index("panel") * count, count)
    now = series[pl.ds(start, count), :].astype(jnp.float32)
    now = now.reshape(count // 16, 2, 8, variables)
    out[...] = jnp.concatenate([now[:, 0], now[:, 1]], 2).reshape(count // 2, 2 * variables).astype(out.dtype)


def place_kernel(plan, *refs):
    stacks = refs[:-3]
    wide, packed, record_sem = refs[-3:]
    i = lax.axis_index("tm")
    panel = lax.axis_index("panel")
    hi, lo = i // plan.lo, i % plan.lo
    count = stacks[0].shape[0] // plan.hi
    total = plan.n * 2 * count

    def record_copy(side, slo, shi):
        slab = (hi ^ shi) * plan.lo + (lo ^ slo)
        first = (slab * 2 + lax.rem(panel + side, 2)) * count
        return pltpu.make_async_copy(
            stacks[side * plan.lo + slo].at[pl.ds(pl.multiple_of(shi * count, count), count), :],
            packed.at[pl.ds(pl.multiple_of(first, count), count), :],
            record_sem.at[(side * plan.lo + slo) * plan.hi + shi],
        )

    for side in range(2):
        for slo in range(plan.lo):

            @pl.loop(0, plan.hi)
            def _(shi):
                record_copy(side, slo, shi).start()

    packed[total:, :] = jnp.zeros((packed.shape[0] - total, packed.shape[1]), packed.dtype)
    for side in range(2):
        for slo in range(plan.lo):

            @pl.loop(0, plan.hi)
            def _(shi):
                record_copy(side, slo, shi).wait()

    step = 128
    lanes = packed.shape[1]
    left = lax.broadcasted_iota(jnp.int32, (step, lanes), 1) < lanes // 2

    @pl.loop(0, wide.shape[0] // (2 * step))
    def _(k):
        start = pl.multiple_of(k * step, step)
        now = packed[pl.ds(start, step + 16), :].astype(jnp.float32)
        turned = pltpu.roll(now, lanes // 2, 1)
        late = jnp.where(left, turned[:step], turned[8 : step + 8])
        both = jnp.stack([now[:step].reshape(step // 8, 8, lanes), late.reshape(step // 8, 8, lanes)], 1)
        wide[pl.ds(pl.multiple_of(k * 2 * step, 2 * step), 2 * step), :] = both.reshape(2 * step, lanes).astype(
            wide.dtype
        )


def sketch_kernel(plan, rows, depth, variables, where, sb, wide, *refs):
    blocks, out = refs[:-1], refs[-1]
    i = lax.axis_index("tm")
    panel = lax.axis_index("panel")
    a, b = plan.coords(i, panel)
    shift = depth // variables * LAG_SPACING
    slab = plan.index(a, b ^ sb, panel)

    @pl.loop(0, rows // TILE)
    def _(k):
        start = pl.multiple_of(k * TILE, TILE)
        acc = jnp.zeros((TILE, out.shape[1]), jnp.float32)
        for sa in range(plan.na):
            block = plan.index(a ^ sa, b, panel)
            base = pl.multiple_of(slab * rows + block * shift + start, 16)
            past = 0
            for array, row, count in where[sa]:
                chunk = min(256, count)
                for first in range(0, count, chunk):
                    pieces = []
                    for col in range(past + first, past + first + chunk, 2 * variables):
                        offset = col // variables * LAG_SPACING
                        pieces.append(wide[pl.ds(base + offset, TILE), :])
                    left = jnp.concatenate(pieces, 1) if len(pieces) > 1 else pieces[0]
                    right = blocks[array][row + first : row + first + chunk, :]
                    acc = acc + jnp.dot(left, right, preferred_element_type=jnp.float32)
                past += count
        out[pl.ds(start, TILE), :] = acc


def gram_kernel(own_ref, other_ref, out_ref):
    half = own_ref.shape[1]
    first, last = own_ref[:, :NB], own_ref[:, NB:]
    out_ref[:, :half] = dot_tn(first, own_ref[...])
    out_ref[:, half : half + NB] = dot_tn(last, last)
    panel = lax.axis_index("panel")

    def cross(left, right):
        both = dot_tn(left, right)
        out_ref[:, half + NB : half + 2 * NB] = both[:NB]
        out_ref[:, half + 2 * NB :] = both[NB:]

    @pl.when(panel == 0)
    def _():
        cross(own_ref[...], other_ref[:, :NB])

    @pl.when(panel == 1)
    def _():
        cross(other_ref[...], own_ref[:, NB:])


def small_factor(block, base, size):
    cols = [jnp.broadcast_to(block[:, base + j : base + j + 1], (size, NB)) for j in range(size)]
    sub = lax.broadcasted_iota(jnp.int32, (size, NB), 0)
    scale = jnp.zeros((size, NB), jnp.float32)
    left, right = block[:, :NB], block[:, NB:]
    for j in range(size):
        pivot = jnp.broadcast_to(cols[j][j : j + 1, :], (size, NB))
        mult = jnp.where(sub > j, cols[j] * (1.0 / pivot), 0.0)
        for k in range(j + 1, size):
            cols[k] = cols[k] - mult * jnp.broadcast_to(cols[j][k : k + 1, :], (size, NB))
        scale = jnp.where(sub == j, pivot, scale)
        if j < size - 1:
            left = left - mult * jnp.broadcast_to(left[j : j + 1, :], (size, NB))
            right = right - mult * jnp.broadcast_to(right[j : j + 1, :], (size, NB))
    inv = lax.rsqrt(scale)
    return jnp.concatenate([left * inv, right * inv], 1)


def diag_factor(w):
    for kb in range(NB // IB):
        end = (kb + 1) * IB
        rows = small_factor(w[kb * IB : end, :], kb * IB, IB)
        w[kb * IB : end, :] = rows
        if end < NB:
            w[end:, :] = w[end:, :] - dot_tn(rows[:, end:NB], rows)


def factor_kernel(factor, gown, gother, sown_hbm, sother_hbm, basis_hbm, tri_hbm, *scratch):
    a, w, r, v, sown, sother, basis_ref, tri_ref, sem = scratch
    own_in = pltpu.make_async_copy(sown_hbm, sown, sem.at[0])
    other_in = pltpu.make_async_copy(sother_hbm, sother, sem.at[1])
    own_in.start()
    other_in.start()
    half = sown.shape[1]
    n = 2 * half
    panel = lax.axis_index("panel")

    def place(first, second):
        for at, piece in ((0, first), (half, second)):
            a[at : at + NB, at : at + half] = piece[:, :half]
            a[at + NB : at + half, at + NB : at + half] = piece[:, half : half + NB]
        for at, piece in ((half, first), (half + NB, second)):
            a[:NB, at : at + NB] = piece[:, half + NB : half + 2 * NB]
            a[NB:half, at : at + NB] = piece[:, half + 2 * NB :]

    @pl.when(panel == 0)
    def _():
        place(gown, gother)

    @pl.when(panel == 1)
    def _():
        place(gother, gown)

    r[...] = jnp.zeros_like(r)
    v[...] = jnp.zeros_like(v)
    ri = lax.broadcasted_iota(jnp.int32, (NB, NB), 0)
    ci = lax.broadcasted_iota(jnp.int32, (NB, NB), 1)
    eye = (ri == ci).astype(jnp.float32)
    for j in range(n // NB):
        js = slice(j * NB, (j + 1) * NB)
        w[:, :NB] = a[js, js]
        w[:, NB:] = eye
        diag_factor(w)
        wj = w[:, NB:]
        r[js, js] = jnp.where(ci >= ri, w[:, :NB], 0.0)
        v[js, js] = wj.T
        if (j + 1) * NB < n:
            rest = slice((j + 1) * NB, n)
            row = dot_nn(wj, a[js, rest])
            r[js, rest] = row
            for i in range(j + 1, n // NB):
                at = (i - j - 1) * NB
                a[i * NB : (i + 1) * NB, i * NB :] = a[i * NB : (i + 1) * NB, i * NB :] - dot_tn(
                    row[:, at : at + NB], row[:, at:]
                )
        if j > 0:
            top = slice(0, j * NB)
            v[top, js] = -dot_nt(dot_nn(v[top, top], r[top, js]), wj)

    @pl.when(panel == 0)
    def _():
        tri_ref[...] = r[:, :half] * (1.0 / factor)

    @pl.when(panel == 1)
    def _():
        tri_ref[...] = r[:, half:] * (1.0 / factor)

    tri_out = pltpu.make_async_copy(tri_ref, tri_hbm, sem.at[2])
    tri_out.start()
    own_in.wait()
    other_in.wait()
    outs = []
    piece = basis_ref.shape[0] // 2
    for part in range(2):
        at = slice(part * piece, (part + 1) * piece)

        @pl.when(panel == 0)
        def _():
            basis_ref[at, :] = dot_nn(sown[at, :], v[:half, :half] * factor)

        @pl.when(panel == 1)
        def _():
            basis_ref[at, :] = dot_nn(sother[at, :], v[:half, half:] * factor) + dot_nn(
                sown[at, :], v[half:, half:] * factor
            )

        outs.append(pltpu.make_async_copy(basis_ref.at[at, :], basis_hbm.at[at, :], sem.at[3 + part]))
        outs[-1].start()
    tri_out.wait()
    for out in outs:
        out.wait()


def vmem(count):
    return [pl.BlockSpec(memory_space=pltpu.VMEM)] * count


def scoped(mebibytes):
    return pltpu.CompilerParams(vmem_limit_bytes=mebibytes << 20)


def anywhere(count):
    return [pl.BlockSpec(memory_space=pl.ANY)] * count


def in_vmem(value):
    return pltpu.with_memory_space_constraint(value, pltpu.VMEM)


def per_device(series, test_matrix):
    n = lax.axis_size("tm")
    plan = Plan(n)
    rows, variables = series.shape
    depth, half = test_matrix.shape
    own_rows = pl.pallas_call(
        pack_kernel,
        out_shape=jax.ShapeDtypeStruct((rows // 4, 2 * variables), jnp.bfloat16),
        in_specs=vmem(1),
        out_specs=vmem(1)[0],
        name="pack",
        compiler_params=scoped(8),
    )(series)
    test_matrix, own_rows = lax.optimization_barrier((test_matrix, own_rows))
    arrays, where = gather_blocks(plan, test_matrix)
    pieces = [own_rows]
    for s in range(1, plan.hi):
        pieces.append(lax.ppermute(own_rows, "tm", plan.plain_pairs(s, 0)))
    stack = jnp.concatenate(pieces, 0)
    stacks = [stack]
    for s in range(1, plan.lo):
        stacks.append(lax.ppermute(stack, "tm", plan.plain_pairs(0, s)))
    if plan.na == 4:
        stacks = lax.optimization_barrier((stacks, arrays[1], arrays[2]))[0]
    stacks = stacks + [lax.ppermute(value, "panel", SWAP) for value in stacks]
    length = n * rows + WINDOW_LAGS * LAG_SPACING
    wide = pl.pallas_call(
        functools.partial(place_kernel, plan),
        out_shape=pltpu.VMEM((length, 2 * variables), jnp.bfloat16),
        in_specs=anywhere(len(stacks)),
        out_specs=vmem(1)[0],
        scratch_shapes=[
            pltpu.VMEM((length // 2 + 16, 2 * variables), jnp.bfloat16),
            pltpu.SemaphoreType.DMA((2 * n,)),
        ],
        name="place",
        compiler_params=scoped(8 + (length * variables * 2 >> 20)),
    )(*stacks)
    wide = in_vmem(wide)
    arrays = [in_vmem(value) for value in arrays]

    def part(sb):
        return pl.pallas_call(
            functools.partial(sketch_kernel, plan, rows, depth, variables, where, sb),
            out_shape=jax.ShapeDtypeStruct((rows, half), jnp.float32),
            in_specs=vmem(1 + len(arrays)),
            out_specs=vmem(1)[0],
            name="sketch%d" % sb,
            compiler_params=scoped(8),
            cost_estimate=pl.CostEstimate(
                flops=2 * rows * plan.na * depth * half, bytes_accessed=4 * rows * half, transcendentals=0
            ),
        )(wide, *arrays)

    own = scatter_sums(plan, part)
    other = lax.ppermute(own, "panel", SWAP)
    assert half == 2 * NB
    width = 5 * NB
    gram = pl.pallas_call(
        gram_kernel,
        out_shape=jax.ShapeDtypeStruct((NB, width), jnp.float32),
        in_specs=vmem(2),
        out_specs=vmem(1)[0],
        name="gram",
        compiler_params=scoped(16),
    )(in_vmem(own), in_vmem(other))
    spread = lax.all_to_all(gram.reshape(n, NB // n, width), "tm", 0, 0, tiled=True)
    summed = jnp.sum(spread, 0)
    alike = jnp.broadcast_to(summed[None], (n, NB // n, width))
    gram = lax.all_to_all(alike, "tm", 0, 0, tiled=True).reshape(NB, width)
    gram_other = lax.ppermute(gram, "panel", SWAP)
    full = 2 * half
    return tuple(
        pl.pallas_call(
            functools.partial(factor_kernel, math.sqrt(n * rows)),
            out_shape=[
                jax.ShapeDtypeStruct((rows, half), jnp.float32),
                jax.ShapeDtypeStruct((full, half), jnp.float32),
            ],
            in_specs=vmem(2) + anywhere(2),
            out_specs=anywhere(2),
            scratch_shapes=[
                pltpu.VMEM((full, full), jnp.float32),
                pltpu.VMEM((NB, 2 * NB), jnp.float32),
                pltpu.VMEM((full, full), jnp.float32),
                pltpu.VMEM((full, full), jnp.float32),
                pltpu.VMEM((rows, half), jnp.float32),
                pltpu.VMEM((rows, half), jnp.float32),
                pltpu.VMEM((rows, half), jnp.float32),
                pltpu.VMEM((full, half), jnp.float32),
                pltpu.SemaphoreType.DMA((5,)),
            ],
            name="factor",
            compiler_params=scoped(24),
        )(gram, gram_other, own, other)
    )


def solution(mesh):
    placed = (P(("grp", "tm"), None), P("tm", "panel"))
    return jax.shard_map(
        per_device,
        mesh=mesh,
        in_specs=placed,
        out_specs=(P(("grp", "tm"), "panel"), P("grp", "panel")),
        check_vma=False,
    )
```

```python
import functools
import math

import jax
import jax.numpy as jnp
import numpy as np
from jax import lax
from jax.experimental import pallas as pl
from jax.experimental.pallas import tpu as pltpu
from jax.sharding import PartitionSpec as P

WINDOW_LAGS = 256
LAG_SPACING = 8
NB = 128
IB = 16
TILE = 256
HI = lax.Precision.HIGHEST
BOTH = ("tm", "panel")
SWAP = [(0, 1), (1, 0)]


def dot_nn(a, b):
    return lax.dot_general(a, b, (((1,), (0,)), ((), ())), precision=HI, preferred_element_type=jnp.float32)


def dot_tn(a, b):
    return lax.dot_general(a, b, (((0,), (0,)), ((), ())), precision=HI, preferred_element_type=jnp.float32)


def dot_nt(a, b):
    return lax.dot_general(a, b, (((1,), (1,)), ((), ())), precision=HI, preferred_element_type=jnp.float32)


def split_stack(value, axis, left):
    high = value.astype(jnp.bfloat16)
    rest = value - high.astype(jnp.float32)
    mid = rest.astype(jnp.bfloat16)
    low = (rest - mid.astype(jnp.float32)).astype(jnp.bfloat16)
    order = [high, high, mid, high, low, mid] if left else [high, mid, high, low, high, mid]
    return jnp.concatenate(order, axis)


def stacked(a_axis, b_axis):
    def product(a, b):
        return lax.dot_general(
            split_stack(a, a_axis, True),
            split_stack(b, b_axis, False),
            (((a_axis,), (b_axis,)), ((), ())),
            preferred_element_type=jnp.float32,
        )

    return product


stack_nn, stack_tn, stack_nt = stacked(1, 0), stacked(0, 0), stacked(1, 1)


class Plan:
    def __init__(self, n):
        assert n & (n - 1) == 0
        lo = 1
        while lo * lo * 4 <= n:
            lo *= 2
        self.n, self.lo, self.hi = n, lo, n // lo
        self.mixed = self.lo == self.hi
        self.na, self.nb = self.hi, self.lo

    def index(self, a, b, panel):
        straight = a * self.lo + b
        if not self.mixed:
            return straight
        return (1 - panel) * (b * self.lo + a) + panel * straight

    def coords(self, i, panel):
        hi, lo = i // self.lo, i % self.lo
        if not self.mixed:
            return hi, lo
        return (1 - panel) * lo + panel * hi, (1 - panel) * hi + panel * lo

    def pairs(self, da, db):
        out = []
        for i in range(self.n):
            for panel in range(2):
                a, b = self.coords(i, panel)
                out.append((i * 2 + panel, self.index(a ^ da, b ^ db, panel) * 2 + panel))
        return out

    def plain_pairs(self, dhi, dlo):
        return [(i, (i // self.lo ^ dhi) * self.lo + (i % self.lo ^ dlo)) for i in range(self.n)]


def gather_blocks(plan, block):
    depth = block.shape[0]

    def sent(value, da):
        return lax.ppermute(value, BOTH, plan.pairs(da, 0))

    if plan.na != 4:
        arrays = [block] + [sent(block, s) for s in range(1, plan.na)]
        return arrays, [[(s, 0, depth)] for s in range(plan.na)]
    cut = depth // 2
    one, two = sent(block, 1), sent(block, 2)
    top, bottom = sent(one[:cut], 2), sent(two[cut:], 1)
    return [block, one, two, top, bottom], [
        [(0, 0, depth)],
        [(1, 0, depth)],
        [(2, 0, depth)],
        [(3, 0, cut), (4, 0, cut)],
    ]


def scatter_sums(plan, part):
    def sent(value, db):
        return lax.ppermute(value, BOTH, plan.pairs(0, db))

    if plan.nb != 4:
        arrived = [sent(part(s), s) for s in range(1, plan.nb)]
        own = part(0)
    else:
        third = part(3)
        cut = third.shape[0] // 2
        top, bottom = sent(third[:cut], 1), sent(third[cut:], 2)
        two, one = part(2), part(1)
        two = jnp.concatenate([two[:cut] + top, two[cut:]], 0)
        one = jnp.concatenate([one[:cut], one[cut:] + bottom], 0)
        arrived = [sent(two, 2), sent(one, 1)]
        own = part(0)
    for piece in arrived:
        own = own + piece
    return own


def pack_kernel(series, out):
    count = 2 * out.shape[0]
    variables = series.shape[1]
    start = pl.multiple_of(lax.axis_index("panel") * count, count)
    now = series[pl.ds(start, count), :].astype(jnp.float32)
    now = now.reshape(count // 16, 2, 8, variables)
    out[...] = jnp.concatenate([now[:, 0], now[:, 1]], 2).reshape(count // 2, 2 * variables).astype(out.dtype)


def place_kernel(plan, *refs):
    stacks = refs[:-3]
    wide, packed, record_sem = refs[-3:]
    i = lax.axis_index("tm")
    panel = lax.axis_index("panel")
    hi, lo = i // plan.lo, i % plan.lo
    count = stacks[0].shape[0] // plan.hi
    total = plan.n * 2 * count

    def record_copy(side, slo, shi):
        slab = (hi ^ shi) * plan.lo + (lo ^ slo)
        first = (slab * 2 + lax.rem(panel + side, 2)) * count
        return pltpu.make_async_copy(
            stacks[side * plan.lo + slo].at[pl.ds(pl.multiple_of(shi * count, count), count), :],
            packed.at[pl.ds(pl.multiple_of(first, count), count), :],
            record_sem.at[(side * plan.lo + slo) * plan.hi + shi],
        )

    for side in range(2):
        for slo in range(plan.lo):

            @pl.loop(0, plan.hi)
            def _(shi):
                record_copy(side, slo, shi).start()

    packed[total:, :] = jnp.zeros((packed.shape[0] - total, packed.shape[1]), packed.dtype)
    for side in range(2):
        for slo in range(plan.lo):

            @pl.loop(0, plan.hi)
            def _(shi):
                record_copy(side, slo, shi).wait()

    step = 512
    lanes = packed.shape[1]
    left = lax.broadcasted_iota(jnp.int32, (step, lanes), 1) < lanes // 2

    @pl.loop(0, wide.shape[0] // (2 * step))
    def _(k):
        start = pl.multiple_of(k * step, step)
        now = packed[pl.ds(start, step + 16), :].astype(jnp.float32)
        turned = pltpu.roll(now, lanes // 2, 1)
        late = jnp.where(left, turned[:step], turned[8 : step + 8])
        both = jnp.stack([now[:step].reshape(step // 8, 8, lanes), late.reshape(step // 8, 8, lanes)], 1)
        wide[pl.ds(pl.multiple_of(k * 2 * step, 2 * step), 2 * step), :] = both.reshape(2 * step, lanes).astype(
            wide.dtype
        )


def sketch_kernel(plan, rows, depth, variables, where, sb, wide, *refs):
    blocks, out = refs[:-1], refs[-1]
    i = lax.axis_index("tm")
    panel = lax.axis_index("panel")
    a, b = plan.coords(i, panel)
    shift = depth // variables * LAG_SPACING
    slab = plan.index(a, b ^ sb, panel)

    @pl.loop(0, rows // TILE)
    def _(k):
        start = pl.multiple_of(k * TILE, TILE)
        acc = jnp.zeros((TILE, out.shape[1]), jnp.float32)
        for sa in range(plan.na):
            block = plan.index(a ^ sa, b, panel)
            base = pl.multiple_of(slab * rows + block * shift + start, 16)
            past = 0
            for array, row, count in where[sa]:
                chunk = min(256, count)
                for first in range(0, count, chunk):
                    pieces = []
                    for col in range(past + first, past + first + chunk, 2 * variables):
                        offset = col // variables * LAG_SPACING
                        pieces.append(wide[pl.ds(base + offset, TILE), :])
                    left = jnp.concatenate(pieces, 1) if len(pieces) > 1 else pieces[0]
                    right = blocks[array][row + first : row + first + chunk, :]
                    acc = acc + jnp.dot(left, right, preferred_element_type=jnp.float32)
                past += count
        out[pl.ds(start, TILE), :] = acc


def gram_kernel(own_ref, other_ref, out_ref):
    half = own_ref.shape[1]
    first, last = own_ref[:, :NB], own_ref[:, NB:]
    out_ref[:, :half] = dot_tn(first, own_ref[...])
    out_ref[:, half : half + NB] = dot_tn(last, last)
    panel = lax.axis_index("panel")

    def cross(left, right):
        both = dot_tn(left, right)
        out_ref[:, half + NB : half + 2 * NB] = both[:NB]
        out_ref[:, half + 2 * NB :] = both[NB:]

    @pl.when(panel == 0)
    def _():
        cross(own_ref[...], other_ref[:, :NB])

    @pl.when(panel == 1)
    def _():
        cross(other_ref[...], own_ref[:, NB:])


def small_factor(block, base, size):
    cols = [jnp.broadcast_to(block[:, base + j : base + j + 1], (size, NB)) for j in range(size)]
    sub = lax.broadcasted_iota(jnp.int32, (size, NB), 0)
    scale = jnp.zeros((size, NB), jnp.float32)
    left, right = block[:, :NB], block[:, NB:]
    for j in range(size):
        pivot = jnp.broadcast_to(cols[j][j : j + 1, :], (size, NB))
        mult = jnp.where(sub > j, cols[j] * (1.0 / pivot), 0.0)
        for k in range(j + 1, size):
            cols[k] = cols[k] - mult * jnp.broadcast_to(cols[j][k : k + 1, :], (size, NB))
        scale = jnp.where(sub == j, pivot, scale)
        if j < size - 1:
            left = left - mult * jnp.broadcast_to(left[j : j + 1, :], (size, NB))
            right = right - mult * jnp.broadcast_to(right[j : j + 1, :], (size, NB))
    inv = lax.rsqrt(scale)
    return jnp.concatenate([left * inv, right * inv], 1)


def diag_factor(w):
    for kb in range(NB // IB):
        end = (kb + 1) * IB
        rows = small_factor(w[kb * IB : end, :], kb * IB, IB)
        w[kb * IB : end, :] = rows
        if end < NB:
            w[end:, :] = w[end:, :] - stack_tn(rows[:, :NB], rows)[end:, :]


def factor_kernel(factor, gown, gother, sown_hbm, sother_hbm, basis_hbm, tri_hbm, *scratch):
    a, w, r, v, sown, sother, basis_ref, tri_ref, sem = scratch
    own_in = pltpu.make_async_copy(sown_hbm, sown, sem.at[0])
    other_in = pltpu.make_async_copy(sother_hbm, sother, sem.at[1])
    own_in.start()
    other_in.start()
    half = sown.shape[1]
    n = 2 * half
    panel = lax.axis_index("panel")

    def place(first, second):
        for at, piece in ((0, first), (half, second)):
            a[at : at + NB, at : at + half] = piece[:, :half]
            a[at + NB : at + half, at + NB : at + half] = piece[:, half : half + NB]
        for at, piece in ((half, first), (half + NB, second)):
            a[:NB, at : at + NB] = piece[:, half + NB : half + 2 * NB]
            a[NB:half, at : at + NB] = piece[:, half + 2 * NB :]

    @pl.when(panel == 0)
    def _():
        place(gown, gother)

    @pl.when(panel == 1)
    def _():
        place(gother, gown)

    r[...] = jnp.zeros_like(r)
    v[...] = jnp.zeros_like(v)
    ri = lax.broadcasted_iota(jnp.int32, (NB, NB), 0)
    ci = lax.broadcasted_iota(jnp.int32, (NB, NB), 1)
    eye = (ri == ci).astype(jnp.float32)
    for j in range(n // NB):
        js = slice(j * NB, (j + 1) * NB)
        w[:, :NB] = a[js, js]
        w[:, NB:] = eye
        diag_factor(w)
        wj = w[:, NB:]
        r[js, js] = jnp.where(ci >= ri, w[:, :NB], 0.0)
        v[js, js] = wj.T
        if (j + 1) * NB < n:
            rest = slice((j + 1) * NB, n)
            row = stack_nn(wj, a[js, rest])
            r[js, rest] = row
            for i in range(j + 1, n // NB):
                at = (i - j - 1) * NB
                a[i * NB : (i + 1) * NB, i * NB :] = a[i * NB : (i + 1) * NB, i * NB :] - stack_tn(
                    row[:, at : at + NB], row[:, at:]
                )
        if j > 0:
            top = slice(0, j * NB)
            v[top, js] = -stack_nt(stack_nn(v[top, top], r[top, js]), wj)

    @pl.when(panel == 0)
    def _():
        tri_ref[...] = r[:, :half] * (1.0 / factor)

    @pl.when(panel == 1)
    def _():
        tri_ref[...] = r[:, half:] * (1.0 / factor)

    tri_out = pltpu.make_async_copy(tri_ref, tri_hbm, sem.at[2])
    tri_out.start()
    own_in.wait()
    other_in.wait()
    outs = []
    piece = basis_ref.shape[0] // 2
    for part in range(2):
        at = slice(part * piece, (part + 1) * piece)

        @pl.when(panel == 0)
        def _():
            basis_ref[at, :] = dot_nn(sown[at, :], v[:half, :half] * factor)

        @pl.when(panel == 1)
        def _():
            basis_ref[at, :] = dot_nn(sother[at, :], v[:half, half:] * factor) + dot_nn(
                sown[at, :], v[half:, half:] * factor
            )

        outs.append(pltpu.make_async_copy(basis_ref.at[at, :], basis_hbm.at[at, :], sem.at[3 + part]))
        outs[-1].start()
    tri_out.wait()
    for out in outs:
        out.wait()


def vmem(count):
    return [pl.BlockSpec(memory_space=pltpu.VMEM)] * count


def scoped(mebibytes):
    return pltpu.CompilerParams(vmem_limit_bytes=mebibytes << 20)


def anywhere(count):
    return [pl.BlockSpec(memory_space=pl.ANY)] * count


def in_vmem(value):
    return pltpu.with_memory_space_constraint(value, pltpu.VMEM)


def per_device(series, test_matrix):
    n = lax.axis_size("tm")
    plan = Plan(n)
    rows, variables = series.shape
    depth, half = test_matrix.shape
    own_rows = pl.pallas_call(
        pack_kernel,
        out_shape=jax.ShapeDtypeStruct((rows // 4, 2 * variables), jnp.bfloat16),
        in_specs=vmem(1),
        out_specs=vmem(1)[0],
        name="pack",
        compiler_params=scoped(8),
    )(series)
    test_matrix, own_rows = lax.optimization_barrier((test_matrix, own_rows))
    arrays, where = gather_blocks(plan, test_matrix)
    pieces = [own_rows]
    for s in range(1, plan.hi):
        pieces.append(lax.ppermute(own_rows, "tm", plan.plain_pairs(s, 0)))
    stack = jnp.concatenate(pieces, 0)
    stacks = [stack]
    for s in range(1, plan.lo):
        stacks.append(lax.ppermute(stack, "tm", plan.plain_pairs(0, s)))
    if plan.na == 4:
        stacks = lax.optimization_barrier((stacks, arrays[1], arrays[2]))[0]
    stacks = stacks + [lax.ppermute(value, "panel", SWAP) for value in stacks]
    length = n * rows + WINDOW_LAGS * LAG_SPACING
    wide = pl.pallas_call(
        functools.partial(place_kernel, plan),
        out_shape=pltpu.VMEM((length, 2 * variables), jnp.bfloat16),
        in_specs=anywhere(len(stacks)),
        out_specs=vmem(1)[0],
        scratch_shapes=[
            pltpu.VMEM((length // 2 + 16, 2 * variables), jnp.bfloat16),
            pltpu.SemaphoreType.DMA((2 * n,)),
        ],
        name="place",
        compiler_params=scoped(8 + (length * variables * 2 >> 20)),
    )(*stacks)
    wide = in_vmem(wide)
    arrays = [in_vmem(value) for value in arrays]

    def part(sb):
        return pl.pallas_call(
            functools.partial(sketch_kernel, plan, rows, depth, variables, where, sb),
            out_shape=jax.ShapeDtypeStruct((rows, half), jnp.float32),
            in_specs=vmem(1 + len(arrays)),
            out_specs=vmem(1)[0],
            name="sketch%d" % sb,
            compiler_params=scoped(8),
            cost_estimate=pl.CostEstimate(
                flops=2 * rows * plan.na * depth * half, bytes_accessed=4 * rows * half, transcendentals=0
            ),
        )(wide, *arrays)

    own = scatter_sums(plan, part)
    other = lax.ppermute(own, "panel", SWAP)
    assert half == 2 * NB
    width = 5 * NB
    gram = pl.pallas_call(
        gram_kernel,
        out_shape=jax.ShapeDtypeStruct((NB, width), jnp.float32),
        in_specs=vmem(2),
        out_specs=vmem(1)[0],
        name="gram",
        compiler_params=scoped(16),
    )(in_vmem(own), in_vmem(other))
    spread = lax.all_to_all(gram.reshape(n, NB // n, width), "tm", 0, 0, tiled=True)
    summed = jnp.sum(spread, 0)
    alike = jnp.broadcast_to(summed[None], (n, NB // n, width))
    gram = lax.all_to_all(alike, "tm", 0, 0, tiled=True).reshape(NB, width)
    gram_other = lax.ppermute(gram, "panel", SWAP)
    full = 2 * half
    return tuple(
        pl.pallas_call(
            functools.partial(factor_kernel, math.sqrt(n * rows)),
            out_shape=[
                jax.ShapeDtypeStruct((rows, half), jnp.float32),
                jax.ShapeDtypeStruct((full, half), jnp.float32),
            ],
            in_specs=vmem(2) + anywhere(2),
            out_specs=anywhere(2),
            scratch_shapes=[
                pltpu.VMEM((full, full), jnp.float32),
                pltpu.VMEM((NB, 2 * NB), jnp.float32),
                pltpu.VMEM((full, full), jnp.float32),
                pltpu.VMEM((full, full), jnp.float32),
                pltpu.VMEM((rows, half), jnp.float32),
                pltpu.VMEM((rows, half), jnp.float32),
                pltpu.VMEM((rows, half), jnp.float32),
                pltpu.VMEM((full, half), jnp.float32),
                pltpu.SemaphoreType.DMA((5,)),
            ],
            name="factor",
            compiler_params=scoped(24),
        )(gram, gram_other, own, other)
    )


def solution(mesh):
    placed = (P(("grp", "tm"), None), P("tm", "panel"))
    return jax.shard_map(
        per_device,
        mesh=mesh,
        in_specs=placed,
        out_specs=(P(("grp", "tm"), "panel"), P("grp", "panel")),
        check_vma=False,
    )
```
